256 devices in a mesh: poles: 4 (over y), grid: 64 (over x, z, core).
Axes of the slice: x: 4, y: 4, z: 8, core: 2. Of those that a mesh axis runs over, the one named last changes fastest.
Arguments:
- inverse_block: float32 [4, 2, 4096, 4096], P('poles', None, 'grid'), as said below
- factor_block: float32 [4, 2, 4096, 512], P('poles', None, 'grid'), may hold values from -16 to 16
- diag_inverse: float32 [4, 2, 512, 512], P('poles', None, 'grid'), may hold values from -6 to 6
- residues: float32 [4, 2], P('poles'), may hold values from -4 to 4
- block_owner: int32 [64], replicated, may hold values from 0 to 63, as said below
- row_count: int32 [64], replicated, may hold values from 1 to 64, 3072 in all
Outputs:
- density_off: float32 [2, 4096, 512], P(None, 'grid')
- density_diag: float32 [2, 512, 512], P(None, 'grid')
The draws below stay inside these ranges and needn't reach their ends.
Inputs may be any that keep to these rules, and one draw needn't show every extreme that they name: block_owner is a permutation: natural ancestor row block b (natural rows b * 64 to b * 64 + 63) sits at block position block_owner[b] of the arrays split over grid. With its rows put back in natural order, each pole's inverse_block (real part and imaginary part each) is a symmetric matrix.
All inputs are finite; a program needn't handle non-finite values.
Results may differ from the reference program's by a relative error of at most 0.00007.
Values sent between devices are 32-bit elements; how exact they have to be, the bound alone decides.
No kernel may reach another device: no remote copies, remote signals or barrier semaphores. Data moves between devices by JAX's collectives and lax.ppermute only.
A program may use at most 128 MiB of HBM per device.

```python
import math
import jax
import jax.numpy as jnp
import numpy as np
from jax import lax

S = 512
RD = 64
NBLK = 64
R = 4096
POLES = 4


def shared_owner(key):
    return jax.random.permutation(jax.random.fold_in(key, 7), NBLK).astype(jnp.int32)


def draw_block_owner(key, part):
    return shared_owner(key)


def draw_inverse_block(key, part):
    owner = shared_owner(key)
    blocks = jnp.arange(NBLK, dtype=jnp.int32)
    inverse_of = jnp.zeros((NBLK,), jnp.int32).at[owner].set(blocks)
    gaussian = jax.random.normal(jax.random.fold_in(key, 11), (POLES, 2, R, R), jnp.float32)
    symmetric = (gaussian + jnp.swapaxes(gaussian, 2, 3)) * (0.5 / R) ** 0.5
    stored = jnp.arange(R, dtype=jnp.int32)
    row_order = inverse_of[stored // RD] * RD + stored % RD
    return symmetric[:, :, row_order, :]


def raised(drawn, stream_key, source, target, parts, factor):
    def block_of(dim):
        return (jnp.arange(drawn.shape[dim]) // (drawn.shape[dim] // parts)).reshape((-1,) + (1,) * (drawn.ndim - 1 - dim))

    first = jax.random.permutation(stream_key, parts)[block_of(target)]
    far = (block_of(target) + parts // 2) % parts
    return jnp.where((block_of(source) == first) | (block_of(source) == far), factor * drawn, drawn)


def levels(stream_key, dims, shards, smallest, high):
    def one(axis_at, shards_of):
        draws = jax.random.uniform(jax.random.fold_in(jax.random.fold_in(stream_key, 6), axis_at), (shards_of,), jnp.float32, smallest / len(shards), high / len(shards))
        return jnp.repeat(jnp.exp(draws), dims[axis_at] // shards_of).reshape((-1,) + (1,) * (len(dims) - axis_at - 1))

    gain = one(*shards[0])
    for cut in shards[1:]:
        gain = gain * one(*cut)
    return gain


def profile(amount, total, limit, slope):
    weights = [(1 << 20) // math.isqrt(rank ** slope) + 1 for rank in range(2, amount + 1)]
    rest, holding = total - limit - (amount - 1), [1] * (amount - 1)
    while rest > 0:
        movable = [i for i in range(amount - 1) if holding[i] < limit]
        pool, remaining = sum([weights[i] for i in movable]), rest
        for i in movable:
            more = min(limit - holding[i], max(1, remaining * weights[i] // pool), rest)
            holding[i] = holding[i] + more
            rest = rest - more
    return np.array([limit] + holding)


def uneven(own_key, amount, total, most, skew):
    if amount == 2:
        one = jax.random.randint(own_key, (), max(1, total - most), min(most, total - 1) + 1)
        return jnp.stack([one, total - one])
    sizes = jnp.asarray(profile(amount, total, most, skew), jnp.int32)
    twos = (amount - 1) // 2
    donor, sink = sizes[1:1 + 2 * twos:2], sizes[2:2 + 2 * twos:2]
    slack = jnp.minimum(donor - 1, most - sink)
    shifted = jax.random.randint(jax.random.fold_in(own_key, 1), (twos,), 0, 1 << 20) % (slack + 1)
    sizes = sizes.at[1:1 + 2 * twos:2].set(donor - shifted).at[2:2 + 2 * twos:2].set(sink + shifted)
    return sizes[jax.random.permutation(jax.random.fold_in(own_key, 2), amount)]


def normal_values(rng, dims, width, reach, shards=(), kind=jnp.bfloat16):
    entries = jax.random.normal(rng, dims, jnp.float32) * width
    if len(shards) > 0:
        entries = levels(rng, dims, shards, -0.22, 0.18) * entries
    return jnp.clip(entries, min=-reach, max=reach).astype(kind)


def heavy_noise(stream_key, extent, deviation, most, cuts, heavy, held_as=jnp.bfloat16):
    entries = deviation * jax.random.normal(stream_key, extent, jnp.float32)
    if cuts:
        entries = entries * levels(stream_key, extent, cuts, -0.22, 0.18)
    return jnp.clip(raised(entries, jax.random.fold_in(stream_key, 3), *heavy), -most, most).astype(held_as)


def setup_inputs(seed: int = 0) -> dict:
    splits = jax.random.split(jax.random.key(seed), 7)
    inverse_block = draw_inverse_block(jax.random.fold_in(splits[6], 71), 0)
    factor_block = heavy_noise(splits[1], (POLES, 2, R, S), 1.0, 16.0, ((0, 4), (2, 64)), (2, 3, 64, 4.0), jnp.float32)
    diag_inverse = normal_values(splits[2], (POLES, 2, S, S), 1.0, 6.0, ((0, 4), (2, 64)), jnp.float32)
    residues = normal_values(splits[3], (POLES, 2), 1.0, 4.0, ((0, 4),), jnp.float32)
    block_owner = draw_block_owner(jax.random.fold_in(splits[6], 71), 0)
    row_count = uneven(splits[5], NBLK, NBLK * RD * 3 // 4, RD, 0).astype(jnp.int32)
    return {"inverse_block": inverse_block, "factor_block": factor_block, "diag_inverse": diag_inverse, "residues": residues, "block_owner": block_owner, "row_count": row_count}


HIGHEST_PRECISION = lax.Precision.HIGHEST


def product(left, right):
    return jnp.dot(left, right, preferred_element_type=jnp.float32, precision=HIGHEST_PRECISION)


def complex_product(left_real, left_imag, right_real, right_imag):
    return (product(left_real, right_real) - product(left_imag, right_imag),
            product(left_real, right_imag) + product(left_imag, right_real))


def weigh(weights, values):
    return jnp.stack([weights[0] * values[0] - weights[1] * values[1],
                      weights[0] * values[1] + weights[1] * values[0]])


def reference(inverse_block, factor_block, diag_inverse, residues, block_owner, row_count):
    blocks = jnp.arange(NBLK, dtype=jnp.int32)
    inverse_of = jnp.zeros((NBLK,), jnp.int32).at[block_owner].set(blocks)
    live_table = (jnp.arange(RD, dtype=jnp.int32)[None, :] < row_count[:, None]).astype(jnp.float32)
    live_rows = live_table[inverse_of].reshape(R)
    masked = factor_block * live_rows[None, None, :, None]
    natural_factor = masked.reshape(POLES, 2, NBLK, RD, S)[:, :, block_owner].reshape(POLES, 2, R, S)

    def one_pole(pole):
        matrix = inverse_block[pole]
        natural_rows = natural_factor[pole]
        masked_rows = masked[pole]
        real_part, imag_part = complex_product(matrix[0], matrix[1], natural_rows[0], natural_rows[1])
        offdiag = -jnp.stack([real_part, imag_part]) * live_rows[None, :, None]
        gram_real, gram_imag = complex_product(masked_rows[0].T, masked_rows[1].T, offdiag[0], offdiag[1])
        diagonal = diag_inverse[pole] - jnp.stack([gram_real, gram_imag])
        return weigh(residues[pole], offdiag), weigh(residues[pole], diagonal)

    offdiags, diagonals = lax.map(one_pole, jnp.arange(POLES, dtype=jnp.int32))
    return jnp.sum(offdiags, axis=0), jnp.sum(diagonals, axis=0)
```

```python
import jax
import jax.numpy as jnp
from jax import lax
from jax.experimental import pallas as pl
from jax.experimental.pallas import tpu as pltpu
from jax.sharding import Mesh, PartitionSpec as P


F32 = jnp.float32
BF16 = jnp.bfloat16
NX, NZ, NK, NY = 4, 8, 2, 4
OFFSETS = (0, 1, -1, 2, -2, 3, -3, 4)

SMEM = pl.BlockSpec(memory_space=pltpu.SMEM)
VMEM = pl.BlockSpec(memory_space=pltpu.VMEM)


def shape(*dims, dtype=F32):
    return jax.ShapeDtypeStruct(dims, dtype)


def call(kernel, out_shape, in_specs, out_specs, scratch, flops, nbytes, *args):
    return pl.pallas_call(
        kernel,
        out_shape=out_shape,
        in_specs=in_specs,
        out_specs=out_specs,
        scratch_shapes=scratch,
        cost_estimate=pl.CostEstimate(flops=flops, bytes_accessed=nbytes, transcendentals=0),
        compiler_params=pltpu.CompilerParams(vmem_limit_bytes=48 << 20),
    )(*args)


def split(value):
    high = value.astype(BF16)
    return high, (value - high.astype(F32)).astype(BF16)


def mask_kernel(place, owner, counts, factor, masked, count):
    def body(b, found):
        return jnp.where(owner[b] == place[3], counts[b], found)

    live = lax.fori_loop(0, 64, body, jnp.int32(0))
    count[0] = live
    rows = lax.broadcasted_iota(jnp.int32, (64, 512), 0)
    keep = rows < live
    for part in range(2):
        masked[part] = jnp.where(keep, factor[part], 0.0)


def columns_kernel(place, owner, inverse, *refs):
    outs, table = refs[:NX], refs[NX]

    def body(b, carry):
        table[owner[b]] = b
        return carry

    lax.fori_loop(0, 64, body, 0)
    x, z, k = place[0], place[1], place[2]
    upper = lax.broadcasted_iota(jnp.int32, (64, 128), 1) // 64
    for dx in range(NX):
        for j, offset in enumerate(OFFSETS):
            for other in range(NK):
                stored = (
                    lax.rem(x + dx, NX) * (NZ * NK)
                    + lax.rem(z + offset + NZ, NZ) * NK
                    + (k + other - 2 * k * other)
                )
                block = table[stored]
                start = pl.multiple_of((block // 2) * 128, 128)
                real = inverse[0, :, pl.ds(start, 128)]
                imag = inverse[1, :, pl.ds(start, 128)]
                same = jnp.where(upper == 0, real, imag)
                cross = pltpu.roll(jnp.where(upper == 0, imag, real), 64, 1)
                t = j * NK + other
                outs[dx][:, t * 128 : (t + 1) * 128] = jnp.where(upper == lax.rem(block, 2), same, cross)


def product_kernel(*refs):
    rows, blocks = refs[:4], refs[4:20]
    outs, (lh, ll) = refs[20:24], refs[24:26]
    xh, xl = refs[26:28]
    lower = lax.broadcasted_iota(jnp.int32, (64, 128), 1) < 64
    for b in range(16):
        for part in range(2):
            high, low = split(blocks[b][part])
            at = b * 128 + part * 64
            lh[at : at + 64, :] = high
            ll[at : at + 64, :] = low
    for i in range(4):
        for t in range(16):
            tile = rows[i][:, t * 128 : (t + 1) * 128]
            lanes = slice(t * 128, (t + 1) * 128)
            for top, value in ((i * 64, jnp.where(lower, tile, -tile)), (256 + i * 64, pltpu.roll(tile, 64, 1))):
                high, low = split(value)
                xh[top : top + 64, lanes] = high
                xl[top : top + 64, lanes] = low
    for n in range(2):
        cols = slice(n * 256, (n + 1) * 256)
        total = jnp.dot(xh[...], lh[:, cols], preferred_element_type=F32)
        total += jnp.dot(xl[...], lh[:, cols], preferred_element_type=F32)
        total += jnp.dot(xh[...], ll[:, cols], preferred_element_type=F32)
        for i in range(4):
            outs[i][0, :, cols] = total[i * 64 : (i + 1) * 64]
            outs[i][1, :, cols] = total[256 + i * 64 : 256 + (i + 1) * 64]


def weigh_kernel(count, weights, p0, p1, p2, p3, weighted, turned):
    rows = lax.broadcasted_iota(jnp.int32, (64, 512), 0)
    keep = rows < count[0]
    real = jnp.where(keep, -(p0[0] + p1[0] + p2[0] + p3[0]), 0.0)
    imag = jnp.where(keep, -(p0[1] + p1[1] + p2[1] + p3[1]), 0.0)
    wr, wi = weights[0], weights[1]
    out_real = wr * real - wi * imag
    out_imag = wr * imag + wi * real
    weighted[0] = out_real
    weighted[1] = out_imag
    both = jnp.concatenate([out_real, out_imag], axis=0).T
    for xc in range(NX):
        for zk in range(NZ * NK):
            at = xc * 128 + zk * 8
            turned[zk, xc * 8 : (xc + 1) * 8, :] = both[at : at + 8, :]


def gram_kernel(place, weights, turned, lh, ll, diag, out, gh, gl):
    z, k = place[1], place[2]
    lower = lax.broadcasted_iota(jnp.int32, (32, 128), 1) < 64
    for j, offset in enumerate(OFFSETS):
        for other in range(NK):
            source = lax.rem(z + offset + NZ, NZ) * NK + (k + other - 2 * k * other)
            tile = turned[source]
            t = j * NK + other
            lanes = slice(t * 128, (t + 1) * 128)
            for top, value in ((0, jnp.where(lower, tile, -tile)), (32, pltpu.roll(tile, 64, 1))):
                high, low = split(value)
                gh[top : top + 32, lanes] = high
                gl[top : top + 32, lanes] = low
    total = jnp.dot(gh[...], lh[...], preferred_element_type=F32)
    total += jnp.dot(gl[...], lh[...], preferred_element_type=F32)
    total += jnp.dot(gh[...], ll[...], preferred_element_type=F32)
    wr, wi = weights[0], weights[1]
    terms = (wr * diag[0] - wi * diag[1], wr * diag[1] + wi * diag[0])
    for xc in range(NX):
        own = (place[0] == xc).astype(F32)
        for part in range(2):
            at = part * 32 + xc * 8
            piece = own * terms[part] - total[at : at + 8, :]
            for y in range(NY):
                out[y * NX + xc, part] = piece


def sum_kernel(pieces, out):
    total = pieces[0]
    for i in range(1, NY * NX):
        total = total + pieces[i]
    out[...] = total


def shift(axis, size, step):
    pairs = [(i, (i + step) % size) for i in range(size)]
    return lambda value: lax.ppermute(value, axis, pairs)


def per_device(inverse_block, factor_block, diag_inverse, residues, block_owner, row_count):
    x, z, k = lax.axis_index("x"), lax.axis_index("z"), lax.axis_index("k")
    place = jnp.stack([x, z, k, (x * NZ + z) * NK + k]).astype(jnp.int32)
    weights = residues[0]

    own, count = call(
        mask_kernel, (shape(2, 64, 512), shape(1, dtype=jnp.int32)),
        [SMEM, SMEM, SMEM, VMEM], (VMEM, SMEM), [], 1 << 16, 1 << 19,
        place, block_owner, row_count, factor_block[0],
    )
    from_above, from_below = shift("z", NZ, -1), shift("z", NZ, 1)
    swap = shift("k", NK, 1)
    ring = {0: own}
    for step in (1, 2, 3):
        ring[step] = from_above(ring[step - 1])
        ring[-step] = from_below(ring[1 - step])
    ring[4] = jnp.concatenate([from_above(ring[3][:1]), from_below(ring[-3][1:])], axis=0)

    pieces = call(
        columns_kernel, (shape(64, 2048),) * NX,
        [SMEM, SMEM, VMEM], (VMEM,) * NX, [pltpu.SMEM((64,), jnp.int32)], 1 << 20, 1 << 22,
        place, block_owner, inverse_block[0],
    )
    rows = [pieces[0]] + [shift("x", NX, dx)(pieces[dx]) for dx in range(1, NX)]

    blocks = []
    for offset in OFFSETS:
        blocks += [ring[offset], swap(ring[offset])]

    *partial, lh, ll = call(
        product_kernel,
        (shape(2, 64, 512),) * 4 + (shape(2048, 512, dtype=BF16),) * 2,
        [VMEM] * 20, (VMEM,) * 6,
        [pltpu.VMEM((512, 2048), BF16)] * 2, 3 << 30, 10 << 20,
        *rows, *blocks,
    )
    homes = [partial[0]] + [shift("x", NX, -dx)(partial[dx]) for dx in range(1, NX)]

    weighted, turned = call(
        weigh_kernel, (shape(2, 64, 512), shape(16, 32, 128)),
        [SMEM, SMEM] + [VMEM] * 4, (VMEM, VMEM), [], 1 << 20, 3 << 19,
        count, weights, *homes,
    )
    others = [shift("y", NY, dy)(weighted) for dy in range(1, NY)]
    density_off = weighted + others[0] + others[1] + others[2]

    turned = lax.all_to_all(turned, ("z", "k"), 0, 0, tiled=True)
    terms = call(
        gram_kernel, shape(16, 2, 8, 512),
        [SMEM, SMEM] + [VMEM] * 4, VMEM,
        [pltpu.VMEM((64, 2048), BF16)] * 2, 1 << 28, 5 << 20,
        place, weights, turned, lh, ll, diag_inverse[0],
    )
    terms = lax.all_to_all(terms, ("y", "x"), 0, 0, tiled=True)
    density_diag = call(
        sum_kernel, shape(2, 8, 512), [VMEM], VMEM, [], 1 << 18, 1 << 19, terms,
    )
    return density_off, density_diag


def solution(mesh):
    inner = Mesh(mesh.devices.reshape(NY, NX, NZ, NK), ("y", "x", "z", "k"))
    grid = ("x", "z", "k")
    placed = (
        P("y", None, grid, None),
        P("y", None, grid, None),
        P("y", None, grid, None),
        P("y", None),
        P(),
        P(),
    )
    return jax.shard_map(
        per_device,
        mesh=inner,
        in_specs=placed,
        out_specs=(P(None, grid, None), P(None, grid, None)),
        check_vma=False,
    )
```

```python
import jax
import jax.numpy as jnp
from jax import lax
from jax.experimental import pallas as pl
from jax.experimental.pallas import tpu as pltpu
from jax.sharding import Mesh, PartitionSpec as P


F32 = jnp.float32
BF16 = jnp.bfloat16
NX, NZ, NK, NY = 4, 8, 2, 4
OFFSETS = (0, 1, -1, 2, -2, 3, -3, 4)

SMEM = pl.BlockSpec(memory_space=pltpu.SMEM)
VMEM = pl.BlockSpec(memory_space=pltpu.VMEM)


def shape(*dims, dtype=F32):
    return jax.ShapeDtypeStruct(dims, dtype)


def call(kernel, out_shape, in_specs, out_specs, scratch, flops, nbytes, *args):
    return pl.pallas_call(
        kernel,
        out_shape=out_shape,
        in_specs=in_specs,
        out_specs=out_specs,
        scratch_shapes=scratch,
        cost_estimate=pl.CostEstimate(flops=flops, bytes_accessed=nbytes, transcendentals=0),
        compiler_params=pltpu.CompilerParams(vmem_limit_bytes=48 << 20),
    )(*args)


def split(value):
    high = value.astype(BF16)
    return high, (value - high.astype(F32)).astype(BF16)


def mask_kernel(table, factor, masked, live):
    x, z, k = table[0, 0], table[0, 1], table[0, 2]
    spots = [(lax.rem(x - r + NX, NX) * NZ + z) * NK + k for r in range(NX)]

    def body(b, found):
        at, rows = table[1, b], table[2, b]
        return tuple(jnp.where(at == spot, rows, have) for spot, have in zip(spots, found))

    counts = lax.fori_loop(0, 64, body, (jnp.int32(0),) * NX)
    for r in range(NX):
        live[r] = counts[r]
    keep = lax.broadcasted_iota(jnp.int32, (64, 512), 0) < counts[0]
    for part in range(2):
        masked[part] = jnp.where(keep, factor[part], 0.0)


def columns_kernel(table, inverse, *refs):
    outs, natural = refs[:NX], refs[NX]

    def body(b, carry):
        natural[table[1, b]] = b
        return carry

    lax.fori_loop(0, 64, body, 0)
    x, z, k = table[0, 0], table[0, 1], table[0, 2]
    upper = lax.broadcasted_iota(jnp.int32, (64, 128), 1) // 64
    for dx in range(NX):
        for j, offset in enumerate(OFFSETS):
            for other in range(NK):
                stored = (
                    lax.rem(x + dx, NX) * (NZ * NK)
                    + lax.rem(z + offset + NZ, NZ) * NK
                    + (k + other - 2 * k * other)
                )
                block = natural[stored]
                start = pl.multiple_of((block // 2) * 128, 128)
                real = inverse[0, :, pl.ds(start, 128)]
                imag = inverse[1, :, pl.ds(start, 128)]
                same = jnp.where(upper == 0, real, imag)
                cross = pltpu.roll(jnp.where(upper == 0, imag, real), 64, 1)
                t = j * NK + other
                outs[dx][:, t * 128 : (t + 1) * 128] = jnp.where(upper == lax.rem(block, 2), same, cross)


def product_kernel(table, *refs):
    rows, blocks, outs = refs[:4], refs[4:20], refs[20:24]
    lh, ll, xh, xl, total = refs[24:]
    lower = lax.broadcasted_iota(jnp.int32, (64, 128), 1) < 64
    for b in range(16):
        for part in range(2):
            high, low = split(blocks[b][part])
            at = b * 128 + part * 64
            lh[at : at + 64, :] = high
            ll[at : at + 64, :] = low
    for i in range(4):
        for t in range(16):
            tile = rows[i][:, t * 128 : (t + 1) * 128]
            lanes = slice(t * 128, (t + 1) * 128)
            for top, value in ((i * 64, jnp.where(lower, tile, -tile)), (256 + i * 64, pltpu.roll(tile, 64, 1))):
                high, low = split(value)
                xh[top : top + 64, lanes] = high
                xl[top : top + 64, lanes] = low
    for n in range(2):
        cols = slice(n * 256, (n + 1) * 256)
        sums = jnp.dot(xh[...], lh[:, cols], preferred_element_type=F32)
        sums += jnp.dot(xl[...], lh[:, cols], preferred_element_type=F32)
        sums += jnp.dot(xh[...], ll[:, cols], preferred_element_type=F32)
        total[:, cols] = sums
    for e in range(NX):
        start = pl.multiple_of(lax.rem(table[0, 0] + e, NX) * 128, 128)
        for i in range(4):
            for part in range(2):
                at = part * 256 + i * 64
                outs[e][part, (e + i) % NX] = total[at : at + 64, pl.ds(start, 128)]


def gram_kernel(table, live, weights, p0, p1, p2, p3, f0, f1, f2, f3, weighted, keep, send, lh, ll, gh, gl, total):
    x, k = table[0, 0], table[0, 2]
    wr, wi = weights[0], weights[1]
    row = lax.broadcasted_iota(jnp.int32, (64, 128), 0)
    lower = lax.broadcasted_iota(jnp.int32, (128, 128), 1) < 64
    for r, factor in enumerate((f0, f1, f2, f3)):
        for part in range(2):
            at = r * 128 + part * 64
            high, low = split(factor[part])
            lh[at : at + 64, :] = high
            ll[at : at + 64, :] = low
        alive = row < live[r]
        real = jnp.where(alive, -(p0[0, r] + p1[0, r] + p2[0, r] + p3[0, r]), 0.0)
        imag = jnp.where(alive, -(p0[1, r] + p1[1, r] + p2[1, r] + p3[1, r]), 0.0)
        out_real = wr * real - wi * imag
        out_imag = wr * imag + wi * real
        home = lax.rem(x - r + NX, NX)
        weighted[home, 0] = out_real
        weighted[home, 1] = out_imag
        tile = jnp.concatenate([out_real, out_imag], axis=0).T
        lanes = slice(r * 128, (r + 1) * 128)
        for top, value in ((0, jnp.where(lower, tile, -tile)), (128, pltpu.roll(tile, 64, 1))):
            high, low = split(value)
            gh[top : top + 128, lanes] = high
            gl[top : top + 128, lanes] = low
    sums = jnp.dot(gh[...], lh[...], preferred_element_type=F32)
    sums += jnp.dot(gl[...], lh[...], preferred_element_type=F32)
    sums += jnp.dot(gh[...], ll[...], preferred_element_type=F32)
    total[...] = sums
    for zc in range(NZ):
        for part in range(2):
            at = part * 128 + zc * 16
            keep[zc, part] = total[pl.ds(pl.multiple_of(at + 8 * k, 8), 8), :]
            send[zc, part] = total[pl.ds(pl.multiple_of(at + 8 - 8 * k, 8), 8), :]


def diagonal_kernel(weights, pieces, diag, out):
    wr, wi = weights[0], weights[1]
    real, imag = diag[0], diag[1]
    terms = (wr * real - wi * imag, wr * imag + wi * real)
    for part in range(2):
        total = pieces[0, part]
        for i in range(1, NZ):
            total = total + pieces[i, part]
        out[part] = terms[part] - total


def shift(axis, size, step):
    pairs = [(i, (i + step) % size) for i in range(size)]

    def go(value):
        return lax.ppermute(value, axis, pairs)

    return go


def per_device(inverse_block, factor_block, diag_inverse, residues, block_owner, row_count):
    x, z, k = lax.axis_index("x"), lax.axis_index("z"), lax.axis_index("k")
    place = jnp.arange(64, dtype=jnp.int32)
    place = jnp.where(place == 0, x, jnp.where(place == 1, z, k)).astype(jnp.int32)
    table = jnp.stack([place, block_owner, row_count])
    weights = residues[0]

    own, live = call(
        mask_kernel, (shape(2, 64, 512), shape(NX, dtype=jnp.int32)),
        [SMEM, VMEM], (VMEM, SMEM), [], 1 << 16, 1 << 19,
        table, factor_block[0],
    )
    pieces = call(
        columns_kernel, (shape(64, 2048),) * NX,
        [SMEM, VMEM], (VMEM,) * NX, [pltpu.SMEM((64,), jnp.int32)], 1 << 20, 1 << 22,
        table, inverse_block[0],
    )
    rows = {0: pieces[0]}
    for dx in (2, 1, 3):
        rows[dx] = shift("x", NX, dx)(pieces[dx])

    ring = {0: own}
    for step in (1, 2, 3):
        ring[step] = shift("z", NZ, -1)(ring[step - 1])
        ring[-step] = shift("z", NZ, 1)(ring[1 - step])
    ring[4] = jnp.concatenate([shift("z", NZ, -1)(ring[3][:1]), shift("z", NZ, 1)(ring[-3][1:])], axis=0)
    blocks = []
    for offset in OFFSETS:
        blocks += [ring[offset], shift("k", NK, 1)(ring[offset])]

    *partial, = call(
        product_kernel,
        (shape(2, NX, 64, 128),) * 4,
        [SMEM] + [VMEM] * 20, (VMEM,) * 4,
        [pltpu.VMEM((2048, 512), BF16)] * 2 + [pltpu.VMEM((512, 2048), BF16)] * 2 + [pltpu.VMEM((512, 512), F32)],
        3 << 30, 10 << 20,
        table, *[rows[dx] for dx in range(NX)], *blocks,
    )
    late, _ = lax.optimization_barrier((own, rows[2]))
    line = [own] + [shift("x", NX, r)(late) for r in range(1, NX)]
    sums = [partial[0]] + [shift("x", NX, e)(partial[e]) for e in range(1, NX)]

    weighted, keep, send = call(
        gram_kernel, (shape(NX, 2, 64, 128), shape(NZ, 2, 8, 512), shape(NZ, 2, 8, 512)),
        [SMEM] * 3 + [VMEM] * 8, (VMEM,) * 3,
        [pltpu.VMEM((512, 512), BF16)] * 2 + [pltpu.VMEM((256, 512), BF16)] * 2 + [pltpu.VMEM((256, 512), F32)],
        1 << 29, 3 << 20,
        table, live, weights, *sums, *line,
    )
    half = keep + shift("k", NK, 1)(send)
    others = [shift("y", NY, dy)(weighted) for dy in range(1, NY)]
    home = weighted + others[0] + others[1] + others[2]
    home = lax.all_to_all(home, "x", 0, 0, tiled=True)
    density_off = home.transpose(1, 2, 0, 3).reshape(2, 64, 512)

    half = lax.all_to_all(half, "z", 0, 0, tiled=True)
    terms = call(
        diagonal_kernel, shape(2, 8, 512), [SMEM, VMEM, VMEM], VMEM, [], 1 << 18, 1 << 19,
        weights, half, diag_inverse[0],
    )
    rest = [shift("y", NY, dy)(terms) for dy in range(1, NY)]
    return density_off, terms + rest[0] + rest[1] + rest[2]


def solution(mesh):
    inner = Mesh(mesh.devices.reshape(NY, NX, NZ, NK), ("y", "x", "z", "k"))
    grid = ("x", "z", "k")
    placed = (
        P("y", None, grid, None),
        P("y", None, grid, None),
        P("y", None, grid, None),
        P("y", None),
        P(),
        P(),
    )

    return jax.shard_map(
        per_device,
        mesh=inner,
        in_specs=placed,
        out_specs=(P(None, grid, None), P(None, grid, None)),
        check_vma=False,
    )
```

```python
import functools

import jax
import jax.numpy as jnp
from jax import lax
from jax.experimental import pallas as pl
from jax.experimental.pallas import tpu as pltpu
from jax.sharding import Mesh, PartitionSpec as P


F32 = jnp.float32
BF16 = jnp.bfloat16
NX, NZ, NK, NY = 4, 8, 2, 4
OFFSETS = (0, 1, -1, 2, -2, 3, -3, 4)

TARGETS = (2, 1, 3, 0)

SMEM = pl.BlockSpec(memory_space=pltpu.SMEM)
HBM = pl.BlockSpec(memory_space=pltpu.HBM)
VMEM = pl.BlockSpec(memory_space=pltpu.VMEM)


def shape(*dims, dtype=F32):
    return jax.ShapeDtypeStruct(dims, dtype)


def call(kernel, out_shape, in_specs, out_specs, scratch, mib, flops, nbytes, *args):
    return pl.pallas_call(
        kernel,
        out_shape=out_shape,
        in_specs=in_specs,
        out_specs=out_specs,
        scratch_shapes=scratch,
        cost_estimate=pl.CostEstimate(flops=flops, bytes_accessed=nbytes, transcendentals=0),
        compiler_params=pltpu.CompilerParams(vmem_limit_bytes=mib << 20),
    )(*args)


def split(value):
    high = value.astype(BF16)
    return high, (value - high.astype(F32)).astype(BF16)


def interleave(upper, odd, real, imag):
    same = jnp.where(upper == 0, real, imag)
    cross = pltpu.roll(jnp.where(upper == 0, imag, real), 64, 1)
    return jnp.where(upper == odd, same, cross)


def other_core(k, other):
    return k + other - 2 * k * other


def lanes_below(limit, rows=64):
    return lax.broadcasted_iota(jnp.int32, (rows, 128), 1) < limit


def one_hot(size, source):
    row = lax.broadcasted_iota(jnp.int32, (size, size), 0)
    column = lax.broadcasted_iota(jnp.int32, (size, size), 1)
    return jnp.where(row == source(column), 1.0, 0.0).astype(BF16)


def mask_kernel(
    owner_hbm, counts_hbm, factor_hbm, own, mine, theirs, live, owner, counts, factor, sems
):
    copies = [
        pltpu.make_async_copy(source, target, sems.at[i])
        for i, (source, target) in enumerate(
            ((owner_hbm, owner), (counts_hbm, counts), (factor_hbm, factor))
        )
    ]
    for copy in copies:
        copy.start()
    x, z, k = lax.axis_index("x"), lax.axis_index("z"), lax.axis_index("k")
    spots = [
        (lax.rem(x - r + NX, NX) * NZ + z) * NK + other_core(k, other) for r in range(NX) for other in range(NK)
    ]
    select = one_hot(128, lambda m: m % 64 // 8 * 16 + other_core(k, m // 64) * 8 + m % 8)
    copies[0].wait()
    copies[1].wait()

    def body(b, found):
        at, rows = owner[b], counts[b]
        return tuple(jnp.where(at == spot, rows, have) for spot, have in zip(spots, found))

    found = lax.fori_loop(0, 64, body, (jnp.int32(0),) * 8, unroll=8)
    for r in range(8):
        live[r] = found[r]
    keep = lax.broadcasted_iota(jnp.int32, (64, 512), 0) < found[0]
    copies[2].wait()
    for part in range(2):
        own[part] = jnp.where(keep, factor[part], 0.0)
    lower = lanes_below(64)
    for part in range(2):
        for q in range(2):
            turned = []
            for target in TARGETS[q * 2 : q * 2 + 2]:
                start = pl.multiple_of(lax.rem(x + target, NX) * 128, 128)
                high, low = split(own[part, :, pl.ds(start, 128)])
                turned.append(
                    jnp.dot(high, select, preferred_element_type=F32) + jnp.dot(low, select, preferred_element_type=F32)
                )
            lanes = slice(q * 128, (q + 1) * 128)
            mine[part, :, lanes] = jnp.where(lower, turned[0], pltpu.roll(turned[1], 64, 1))
            theirs[part, :, lanes] = jnp.where(lower, pltpu.roll(turned[0], 64, 1), turned[1])


def columns_kernel(owner_hbm, inverse_hbm, *refs):
    outs, (owner, natural, inverse, made, sems) = refs[:NX], refs[NX:]
    read = pltpu.make_async_copy(owner_hbm, owner, sems.at[0])
    fill = pltpu.make_async_copy(inverse_hbm, inverse, sems.at[1])
    fill.start()
    read.start()
    read.wait()

    def body(b, carry):
        natural[owner[b]] = b
        return carry

    lax.fori_loop(0, 64, body, 0, unroll=8)
    x, z, k = lax.axis_index("x"), lax.axis_index("z"), lax.axis_index("k")
    upper = lax.broadcasted_iota(jnp.int32, (64, 128), 1) // 64
    fill.wait()
    writes = []
    for dx in (2, 1, 3, 0):
        for j, offset in enumerate(OFFSETS):
            for other in range(NK):
                stored = (
                    lax.rem(x + dx, NX) * (NZ * NK) + lax.rem(z + offset + NZ, NZ) * NK + other_core(k, other)
                )
                block = natural[stored]
                start = pl.multiple_of((block // 2) * 128, 128)
                t = j * NK + other
                made[dx, :, t * 128 : (t + 1) * 128] = interleave(
                    upper, lax.rem(block, 2), inverse[0, :, pl.ds(start, 128)], inverse[1, :, pl.ds(start, 128)]
                )
        writes.append(pltpu.make_async_copy(made.at[dx], outs[dx], sems.at[2 + dx]))
        writes[-1].start()
    for write in writes:
        write.wait()


def rows_kernel(*refs):
    pieces, (xh, xl) = refs[:8], refs[8:]
    for i in range(8):
        for t in range(16):
            at = t if i % 2 == 0 else t + 1 - 2 * (t % 2)
            high, low = split(pieces[i][:, at * 128 : (at + 1) * 128])
            xh[i * 64 : (i + 1) * 64, t * 128 : (t + 1) * 128] = high
            xl[i * 64 : (i + 1) * 64, t * 128 : (t + 1) * 128] = low


def product_kernel(group, xh, xl, *refs):
    blocks, outs = refs[:16], refs[16:18]
    rh, rl, total = refs[18:]
    lanes = slice(group * 128, (group + 1) * 128)
    for t in range(16):
        rows_real, rows_imag = slice(t * 128, t * 128 + 64), slice(t * 128 + 64, t * 128 + 128)
        (real_h, real_l), (imag_h, imag_l) = split(blocks[t][0, :, lanes]), split(blocks[t][1, :, lanes])
        for out, re, im in ((rh, real_h, imag_h), (rl, real_l, imag_l)):
            out[rows_real, 0:128] = re
            out[rows_real, 128:256] = im
            out[rows_imag, 0:128] = -im
            out[rows_imag, 128:256] = re
    sums = jnp.dot(xh[...], rh[...], preferred_element_type=F32)
    sums += jnp.dot(xl[...], rh[...], preferred_element_type=F32)
    sums += jnp.dot(xh[...], rl[...], preferred_element_type=F32)
    total[...] = sums
    lower = lanes_below(64)
    for i in range(8):
        real = total[i * 64 : (i + 1) * 64, 0:128]
        imag = total[i * 64 : (i + 1) * 64, 128:256]
        for half, value in enumerate(
            (jnp.where(lower, real, pltpu.roll(imag, 64, 1)), jnp.where(lower, pltpu.roll(real, 64, 1), imag))
        ):
            e = TARGETS[group * 2 + half]
            outs[half][(e + i // 2) % NX * 2 + i % 2] = value


def line_kernel(*refs):
    factors, (rh, rl) = refs[:8], refs[8:]
    for i in range(8):
        for part in range(2):
            high, low = split(factors[i][part])
            rh[i * 64 : (i + 1) * 64, part * 512 : (part + 1) * 512] = high
            rl[i * 64 : (i + 1) * 64, part * 512 : (part + 1) * 512] = low


def gram_kernel(live, weights, p0, p1, p2, p3, rh, rl, weighted, keep, send, gh, gl, total):
    x, z, k = lax.axis_index("x"), lax.axis_index("z"), lax.axis_index("k")
    wr, wi = weights[0], weights[1]
    row = lax.broadcasted_iota(jnp.int32, (64, 128), 0)
    lower = lanes_below(64)
    for r in range(NX):
        tiles = []
        for other in range(NK):
            i = r * 2 + other
            value = jnp.where(row < live[i], -(p0[i] + p1[i] + p2[i] + p3[i]), 0.0)
            turned = pltpu.roll(value, 64, 1)
            value = wr * value + wi * jnp.where(lower, -turned, turned)
            home = lax.rem(x - r + NX, NX) * NK + other_core(k, other)
            for y in range(NY):
                weighted[y * 8 + home] = value
            tiles.append(value)
        high, low = split(jnp.concatenate(tiles, axis=0).T)
        gh[:, r * 128 : (r + 1) * 128] = high
        gl[:, r * 128 : (r + 1) * 128] = low
    halves = []
    for part in range(2):
        cols = slice(part * 512, (part + 1) * 512)
        sums = jnp.dot(gh[...], rh[:, cols], preferred_element_type=F32)
        sums += jnp.dot(gl[...], rh[:, cols], preferred_element_type=F32)
        sums += jnp.dot(gh[...], rl[:, cols], preferred_element_type=F32)
        halves.append(sums)
    total[0] = halves[0][:64] - halves[1][64:]
    total[1] = halves[1][:64] + halves[0][64:]
    odd = lax.rem(z, 2)
    for h in range(4):
        for part in range(2):
            keep[h, part] = total[part, pl.ds(pl.multiple_of(h * 16 + odd * 8, 8), 8), :]
            send[h, part] = total[part, pl.ds(pl.multiple_of(h * 16 + 8 - odd * 8, 8), 8), :]


def pair_kernel(keep, got, *outs):
    h = lax.axis_index("z") // 2
    for d in range(4):
        at = lax.rem(h + d, 4)
        outs[d][...] = keep[at] + got[at]


def diagonal_kernel(weights, s0, s1, s2, s3, diag, out):
    wr, wi = weights[0], weights[1]
    real, imag = diag[0], diag[1]
    terms = (wr * real - wi * imag, wr * imag + wi * real)
    for part in range(2):
        out[part] = terms[part] - (s0[part] + s1[part] + s2[part] + s3[part])


def home_kernel(pieces, out):
    select = one_hot(256, lambda m: m // 8 % 2 * 128 + m // 128 * 64 + m % 128 // 16 * 8 + m % 8)
    rows = []
    for x in range(NX):
        cores = []
        for k in range(NK):
            i = x * NK + k
            cores.append((pieces[i] + pieces[8 + i]) + (pieces[16 + i] + pieces[24 + i]))
        rows.append(jnp.concatenate(cores, axis=1))
    value = jnp.concatenate(rows, axis=0)
    high, rest = value.astype(BF16), None
    rest = value - high.astype(F32)
    middle, low = split(rest)
    total = jnp.dot(low, select, preferred_element_type=F32)
    total += jnp.dot(middle, select, preferred_element_type=F32)
    total += jnp.dot(high, select, preferred_element_type=F32)
    for x in range(NX):
        for part in range(2):
            out[part, :, x * 128 : (x + 1) * 128] = total[x * 64 : (x + 1) * 64, part * 128 : (part + 1) * 128]


def permute(axis, pairs):
    def go(value):
        return lax.ppermute(value, axis, pairs)

    return go


def shift(axis, size, step):
    return permute(axis, [(i, (i + step) % size) for i in range(size)])


def swap():
    return shift("k", NK, 1)


def per_device(inverse_block, factor_block, diag_inverse, residues, block_owner, row_count):
    weights = residues[0]
    own, mine, theirs, live = call(
        mask_kernel,
        (shape(2, 64, 512), shape(2, 64, 256), shape(2, 64, 256), shape(8, dtype=jnp.int32)),
        [HBM] * 3, (VMEM,) * 3 + (SMEM,),
        [pltpu.SMEM((64,), jnp.int32)] * 2 + [pltpu.VMEM((2, 64, 512), F32), pltpu.SemaphoreType.DMA((3,))],
        60, 1 << 20, 1 << 20,
        block_owner, row_count, factor_block[0],
    )
    chunks = [{0: mine}, {0: swap()(theirs)}]
    for chunk in chunks:
        for step in (1, 2, 3):
            chunk[step] = shift("z", NZ, -1)(chunk[step - 1])
            chunk[-step] = shift("z", NZ, 1)(chunk[1 - step])
    chunks[0][4] = shift("z", NZ, -1)(chunks[0][3])
    chunks[1][4] = shift("z", NZ, 1)(chunks[1][-3])
    blocks = [chunks[c][offset] for offset in OFFSETS for c in range(2)]

    pieces = call(
        columns_kernel, (shape(64, 2048),) * NX, [HBM] * 2, (HBM,) * NX,
        [pltpu.SMEM((64,), jnp.int32)] * 2
        + [pltpu.VMEM((2, 64, 4096), F32), pltpu.VMEM((NX, 64, 2048), F32), pltpu.SemaphoreType.DMA((6,))],
        60, 1 << 20, 4 << 20,
        block_owner, inverse_block[0],
    )
    rows = {0: pieces[0]}
    for dx in (2, 1, 3):
        rows[dx] = shift("x", NX, dx)(pieces[dx])
    both = []
    for dx in range(NX):
        both += [rows[dx], swap()(rows[dx])]
    xh, xl = call(
        rows_kernel, (shape(512, 2048, dtype=BF16),) * 2, [VMEM] * 8, (VMEM,) * 2, [], 16, 1 << 22, 8 << 20, *both,
    )
    sums = {}
    for group in range(2):
        partial = call(
            functools.partial(product_kernel, group), (shape(8, 64, 128),) * 2,
            [VMEM] * 18, (VMEM,) * 2,
            [pltpu.VMEM((2048, 256), BF16)] * 2 + [pltpu.VMEM((512, 256), F32)],
            12, 3 << 29, 6 << 20,
            xh, xl, *blocks,
        )
        for half in range(2):
            e = TARGETS[group * 2 + half]
            sums[e] = shift("x", NX, e)(partial[half]) if e else partial[half]

    late, _ = lax.optimization_barrier((own, rows[2]))
    line = [own] + [shift("x", NX, r)(late) for r in range(1, NX)]
    factors = []
    for r in range(NX):
        factors += [line[r], swap()(line[r])]
    rh, rl = call(
        line_kernel, (shape(512, 1024, dtype=BF16),) * 2, [VMEM] * 8, (VMEM,) * 2, [], 8, 1 << 22, 4 << 20, *factors,
    )
    weighted, keep, send = call(
        gram_kernel, (shape(32, 64, 128), shape(4, 2, 8, 512), shape(4, 2, 8, 512)),
        [SMEM] * 2 + [VMEM] * 6, (VMEM,) * 3,
        [pltpu.VMEM((128, 512), BF16)] * 2 + [pltpu.VMEM((2, 64, 512), F32)], 8, 1 << 29, 4 << 20,
        live, weights, *[sums[e] for e in range(NX)], rh, rl,
    )
    got = permute("z", [(i, i ^ 1) for i in range(NZ)])(send)
    quads = call(
        pair_kernel, (shape(2, 8, 512),) * 4, [VMEM] * 2, (VMEM,) * 4, [], 4, 1 << 17, 1 << 19, keep, got,
    )
    quads = [quads[0]] + [shift("z", NZ, 2 * d)(quads[d]) for d in range(1, 4)]
    terms = call(
        diagonal_kernel, shape(2, 8, 512), [SMEM] + [VMEM] * 5, VMEM, [], 4, 1 << 18, 1 << 19,
        weights, *quads, diag_inverse[0],
    )
    rest = [shift("y", NY, dy)(terms) for dy in range(1, NY)]
    density_diag = (terms + rest[0]) + (rest[1] + rest[2])

    home = lax.all_to_all(weighted, ("y", "x", "k"), 0, 0, tiled=True)
    density_off = call(home_kernel, shape(2, 64, 512), [VMEM], VMEM, [], 8, 1 << 18, 3 << 19, home)
    return density_off, density_diag


def solution(mesh):
    inner = Mesh(mesh.devices.reshape(NY, NX, NZ, NK), ("y", "x", "z", "k"))
    grid = ("x", "z", "k")
    placed = (
        P("y", None, grid, None),
        P("y", None, grid, None),
        P("y", None, grid, None),
        P("y", None),
        P(),
        P(),
    )

    return jax.shard_map(
        per_device,
        mesh=inner,
        in_specs=placed,
        out_specs=(P(None, grid, None), P(None, grid, None)),
        check_vma=False,
    )
```

```python
import functools

import jax
import jax.numpy as jnp
from jax import lax
from jax.experimental import pallas as pl
from jax.experimental.pallas import tpu as pltpu
from jax.sharding import Mesh, PartitionSpec as P


F32 = jnp.float32
BF16 = jnp.bfloat16
NX, NZ, NK, NY = 4, 8, 2, 4
OFFSETS = (0, 1, -1, 2, -2, 3, -3, 4)

TARGETS = (2, 1, 3, 0)
COLUMNS, TILES = 14 * 128, 8 * 128

SMEM = pl.BlockSpec(memory_space=pltpu.SMEM)
HBM = pl.BlockSpec(memory_space=pltpu.HBM)
VMEM = pl.BlockSpec(memory_space=pltpu.VMEM)


def shape(*dims, dtype=F32):
    return jax.ShapeDtypeStruct(dims, dtype)


def call(kernel, out_shape, in_specs, out_specs, scratch, mib, flops, nbytes, *args):
    return pl.pallas_call(
        kernel,
        out_shape=out_shape,
        in_specs=in_specs,
        out_specs=out_specs,
        scratch_shapes=scratch,
        cost_estimate=pl.CostEstimate(flops=flops, bytes_accessed=nbytes, transcendentals=0),
        compiler_params=pltpu.CompilerParams(vmem_limit_bytes=mib << 20),
    )(*args)


def split(value):
    high = value.astype(BF16)
    return high, (value - high.astype(F32)).astype(BF16)


def interleave(upper, odd, real, imag):
    same = jnp.where(upper == 0, real, imag)
    cross = pltpu.roll(jnp.where(upper == 0, imag, real), 64, 1)
    return jnp.where(upper == odd, same, cross)


def other_core(k, other):
    return k + other - 2 * k * other


def lanes_below(limit, rows=64):
    return lax.broadcasted_iota(jnp.int32, (rows, 128), 1) < limit


def one_hot(size, source):
    row = lax.broadcasted_iota(jnp.int32, (size, size), 0)
    column = lax.broadcasted_iota(jnp.int32, (size, size), 1)
    return jnp.where(row == source(column), 1.0, 0.0).astype(BF16)


def mask_kernel(
    owner_hbm, counts_hbm, factor_hbm, own, mine, theirs, live, owner, counts, factor, sems
):
    copies = [
        pltpu.make_async_copy(source, target, sems.at[i])
        for i, (source, target) in enumerate(
            ((owner_hbm, owner), (counts_hbm, counts), (factor_hbm, factor))
        )
    ]
    for copy in copies:
        copy.start()
    x, z, k = lax.axis_index("x"), lax.axis_index("z"), lax.axis_index("k")
    spots = [
        (lax.rem(x - r + NX, NX) * NZ + z) * NK + other_core(k, other) for r in range(NX) for other in range(NK)
    ]
    select = one_hot(128, lambda m: m % 64 // 8 * 16 + other_core(k, m // 64) * 8 + m % 8)
    copies[0].wait()
    copies[1].wait()

    def body(b, found):
        at, rows = owner[b], counts[b]
        return tuple(jnp.where(at == spot, rows, have) for spot, have in zip(spots, found))

    found = lax.fori_loop(0, 64, body, (jnp.int32(0),) * 8, unroll=8)
    for r in range(8):
        live[r] = found[r]
    keep = lax.broadcasted_iota(jnp.int32, (64, 512), 0) < found[0]
    copies[2].wait()
    for part in range(2):
        own[part] = jnp.where(keep, factor[part], 0.0)
    lower = lanes_below(64)
    for part in range(2):
        for q in range(2):
            turned = []
            for target in TARGETS[q * 2 : q * 2 + 2]:
                start = pl.multiple_of(lax.rem(x + target, NX) * 128, 128)
                high, low = split(own[part, :, pl.ds(start, 128)])
                turned.append(
                    jnp.dot(high, select, preferred_element_type=F32) + jnp.dot(low, select, preferred_element_type=F32)
                )
            lanes = slice(q * 128, (q + 1) * 128)
            mine[part, :, lanes] = jnp.where(lower, turned[0], pltpu.roll(turned[1], 64, 1))
            theirs[part, :, lanes] = jnp.where(lower, pltpu.roll(turned[0], 64, 1), turned[1])


def merge_kernel(first, second, out):
    out[0] = first[...]
    out[1] = second[...]


def columns_kernel(owner_hbm, inverse_hbm, *refs):
    outs, (owner, natural, inverse, made, sems) = refs[:NX], refs[NX:]
    read = pltpu.make_async_copy(owner_hbm, owner, sems.at[0])
    fill = pltpu.make_async_copy(inverse_hbm, inverse, sems.at[1])
    fill.start()
    read.start()
    read.wait()

    def body(b, carry):
        natural[owner[b]] = b
        return carry

    lax.fori_loop(0, 64, body, 0, unroll=8)
    x, z, k = lax.axis_index("x"), lax.axis_index("z"), lax.axis_index("k")
    upper = lax.broadcasted_iota(jnp.int32, (64, 128), 1) // 64
    lower = lanes_below(64)

    def tile(dx, offset, other):
        stored = lax.rem(x + dx, NX) * (NZ * NK) + lax.rem(z + offset + NZ, NZ) * NK + other_core(k, other)
        block = natural[stored]
        start = pl.multiple_of((block // 2) * 128, 128)
        return interleave(
            upper, lax.rem(block, 2), inverse[0, :, pl.ds(start, 128)], inverse[1, :, pl.ds(start, 128)]
        )

    fill.wait()
    writes = []
    for dx in (1, 3, 2, 0):
        for j, offset in enumerate(OFFSETS[1:]):
            for other in range(NK):
                t = j * NK + other
                made[dx, :, t * 128 : (t + 1) * 128] = tile(dx, offset, other)
        if dx == 0:
            for r in range(NX):
                both = jnp.concatenate([tile(NX - r, 0, other) for other in range(NK)], axis=0).T
                at = COLUMNS + r * 256
                made[0, :, at : at + 128] = jnp.where(lower, both[:64], pltpu.roll(both[64:], 64, 1))
                made[0, :, at + 128 : at + 256] = jnp.where(lower, pltpu.roll(both[:64], 64, 1), both[64:])
        source = made.at[dx] if dx == 0 else made.at[dx, :, pl.ds(0, COLUMNS)]
        writes.append(pltpu.make_async_copy(source, outs[dx], sems.at[2 + dx]))
        writes[-1].start()
    for write in writes:
        write.wait()


def halve_rows(pieces, xh, xl, first):
    for i, piece in enumerate(pieces):
        rows = slice((first + i) * 64, (first + i + 1) * 64)
        for t in range(2, 16):
            at = (t if i % 2 == 0 else t + 1 - 2 * (t % 2)) - 2
            high, low = split(piece[:, at * 128 : (at + 1) * 128])
            xh[rows, t * 128 : (t + 1) * 128] = high
            xl[rows, t * 128 : (t + 1) * 128] = low


def own_rows_kernel(own, mate, xh, xl, th, tl):
    halve_rows((own, mate), xh, xl, 0)
    for block in range(8):
        rows = slice(block * 64, (block + 1) * 64)
        for t, (source, tile) in enumerate(((own, block), (mate, block + 1 - 2 * (block % 2)))):
            at = COLUMNS + tile * 128
            high, low = split(source[:, at : at + 128])
            th[rows, t * 128 : (t + 1) * 128] = high
            tl[rows, t * 128 : (t + 1) * 128] = low


def rows_kernel(own_h, own_l, tiles_h, tiles_l, *refs):
    pieces, (xh, xl) = refs[:6], refs[6:]
    for out, own, tiles in ((xh, own_h, tiles_h), (xl, own_l, tiles_l)):
        out[0:128, 256:2048] = own[:, 256:2048]
        out[:, 0:256] = tiles[...]
    halve_rows(pieces, xh, xl, 2)


def product_kernel(group, xh, xl, *refs):
    blocks, outs = refs[:9], refs[9:11]
    rh, rl, total = refs[11:]
    lanes = slice(group * 128, (group + 1) * 128)
    for t in range(16):
        rows_real, rows_imag = slice(t * 128, t * 128 + 64), slice(t * 128 + 64, t * 128 + 128)
        block = blocks[t // 2].at[t % 2] if t < 14 else blocks[t - 7].at[0]
        (real_h, real_l), (imag_h, imag_l) = split(block[0, :, lanes]), split(block[1, :, lanes])
        for out, re, im in ((rh, real_h, imag_h), (rl, real_l, imag_l)):
            out[rows_real, 0:128] = re
            out[rows_real, 128:256] = im
            out[rows_imag, 0:128] = -im
            out[rows_imag, 128:256] = re
    sums = jnp.dot(xh[...], rh[...], preferred_element_type=F32)
    sums += jnp.dot(xl[...], rh[...], preferred_element_type=F32)
    sums += jnp.dot(xh[...], rl[...], preferred_element_type=F32)
    total[...] = sums
    lower = lanes_below(64)
    for i in range(8):
        real = total[i * 64 : (i + 1) * 64, 0:128]
        imag = total[i * 64 : (i + 1) * 64, 128:256]
        for half, value in enumerate(
            (jnp.where(lower, real, pltpu.roll(imag, 64, 1)), jnp.where(lower, pltpu.roll(real, 64, 1), imag))
        ):
            e = TARGETS[group * 2 + half]
            outs[half][(e + i // 2) % NX * 2 + i % 2] = value


def line_kernel(*refs):
    factors, (rh, rl) = refs[:8], refs[8:]
    for i in range(8):
        for part in range(2):
            high, low = split(factors[i][part])
            rh[i * 64 : (i + 1) * 64, part * 512 : (part + 1) * 512] = high
            rl[i * 64 : (i + 1) * 64, part * 512 : (part + 1) * 512] = low


def gram_kernel(live, weights, p0, p1, p2, p3, rh, rl, weighted, keep, send, gh, gl, total):
    x, z, k = lax.axis_index("x"), lax.axis_index("z"), lax.axis_index("k")
    wr, wi = weights[0], weights[1]
    row = lax.broadcasted_iota(jnp.int32, (64, 128), 0)
    lower = lanes_below(64)
    for r in range(NX):
        tiles = []
        for other in range(NK):
            i = r * 2 + other
            value = jnp.where(row < live[i], -(p0[i] + p1[i] + p2[i] + p3[i]), 0.0)
            turned = pltpu.roll(value, 64, 1)
            value = wr * value + wi * jnp.where(lower, -turned, turned)
            home = lax.rem(x - r + NX, NX) * NK + other_core(k, other)
            for y in range(NY):
                weighted[y * 8 + home] = value
            tiles.append(value)
        high, low = split(jnp.concatenate(tiles, axis=0).T)
        gh[:, r * 128 : (r + 1) * 128] = high
        gl[:, r * 128 : (r + 1) * 128] = low
    halves = []
    for part in range(2):
        cols = slice(part * 512, (part + 1) * 512)
        sums = jnp.dot(gh[...], rh[:, cols], preferred_element_type=F32)
        sums += jnp.dot(gl[...], rh[:, cols], preferred_element_type=F32)
        sums += jnp.dot(gh[...], rl[:, cols], preferred_element_type=F32)
        halves.append(sums)
    total[0] = halves[0][:64] - halves[1][64:]
    total[1] = halves[1][:64] + halves[0][64:]
    odd = lax.rem(z, 2)
    for h in range(4):
        for part in range(2):
            keep[h, part] = total[part, pl.ds(pl.multiple_of(h * 16 + odd * 8, 8), 8), :]
            send[h, part] = total[part, pl.ds(pl.multiple_of(h * 16 + 8 - odd * 8, 8), 8), :]


def pair_kernel(keep, got, *outs):
    h = lax.axis_index("z") // 2
    for d in range(4):
        at = lax.rem(h + d, 4)
        outs[d][...] = keep[at] + got[at]


def diagonal_kernel(weights, s0, s1, s2, s3, diag, out):
    wr, wi = weights[0], weights[1]
    real, imag = diag[0], diag[1]
    terms = (wr * real - wi * imag, wr * imag + wi * real)
    for part in range(2):
        out[part] = terms[part] - (s0[part] + s1[part] + s2[part] + s3[part])


def home_kernel(pieces, out):
    select = one_hot(256, lambda m: m // 8 % 2 * 128 + m // 128 * 64 + m % 128 // 16 * 8 + m % 8)
    rows = []
    for x in range(NX):
        cores = []
        for k in range(NK):
            i = x * NK + k
            cores.append((pieces[i] + pieces[8 + i]) + (pieces[16 + i] + pieces[24 + i]))
        rows.append(jnp.concatenate(cores, axis=1))
    value = jnp.concatenate(rows, axis=0)
    high, rest = value.astype(BF16), None
    rest = value - high.astype(F32)
    middle, low = split(rest)
    total = jnp.dot(low, select, preferred_element_type=F32)
    total += jnp.dot(middle, select, preferred_element_type=F32)
    total += jnp.dot(high, select, preferred_element_type=F32)
    for x in range(NX):
        for part in range(2):
            out[part, :, x * 128 : (x + 1) * 128] = total[x * 64 : (x + 1) * 64, part * 128 : (part + 1) * 128]


def permute(axis, pairs):
    def go(value):
        return lax.ppermute(value, axis, pairs)

    return go


def shift(axis, size, step):
    return permute(axis, [(i, (i + step) % size) for i in range(size)])


def swap():
    return shift("k", NK, 1)


def per_device(inverse_block, factor_block, diag_inverse, residues, block_owner, row_count):
    weights = residues[0]
    own, mine, theirs, live = call(
        mask_kernel,
        (shape(2, 64, 512), shape(2, 64, 256), shape(2, 64, 256), shape(8, dtype=jnp.int32)),
        [HBM] * 3, (VMEM,) * 3 + (SMEM,),
        [pltpu.SMEM((64,), jnp.int32)] * 2 + [pltpu.VMEM((2, 64, 512), F32), pltpu.SemaphoreType.DMA((3,))],
        60, 1 << 20, 1 << 20,
        block_owner, row_count, factor_block[0],
    )
    ring = {
        0: call(merge_kernel, shape(2, 2, 64, 256), [VMEM] * 2, VMEM, [], 4, 1 << 10, 1 << 19, mine, swap()(theirs))
    }
    for step in (1, 2, 3):
        ring[step] = shift("z", NZ, -1)(ring[step - 1])
        ring[-step] = shift("z", NZ, 1)(ring[1 - step])
    last = [shift("z", NZ, -1)(ring[3][:1]), shift("z", NZ, 1)(ring[-3][1:])]
    blocks = [ring[offset] for offset in OFFSETS[:-1]] + last

    pieces = call(
        columns_kernel,
        tuple(shape(64, COLUMNS + (0 if dx else TILES)) for dx in range(NX)),
        [HBM] * 2, (HBM,) * NX,
        [pltpu.SMEM((64,), jnp.int32)] * 2
        + [pltpu.VMEM((2, 64, 4096), F32), pltpu.VMEM((NX, 64, COLUMNS + TILES), F32)]
        + [pltpu.SemaphoreType.DMA((6,))],
        60, 1 << 20, 5 << 20,
        block_owner, inverse_block[0],
    )
    rows = {0: pieces[0]}
    for dx in (1, 3, 2):
        rows[dx] = shift("x", NX, dx)(pieces[dx])
    both = []
    for dx in range(NX):
        both += [rows[dx], swap()(rows[dx])]
    halves = call(
        own_rows_kernel, (shape(128, 2048, dtype=BF16),) * 2 + (shape(512, 256, dtype=BF16),) * 2,
        [VMEM] * 2, (VMEM,) * 4, [], 4, 1 << 20, 3 << 20, *both[:2],
    )
    xh, xl = call(
        rows_kernel, (shape(512, 2048, dtype=BF16),) * 2, [VMEM] * 10, (VMEM,) * 2, [], 16, 1 << 22, 8 << 20,
        *halves, *both[2:],
    )
    sums = {}
    for group in range(2):
        partial = call(
            functools.partial(product_kernel, group), (shape(8, 64, 128),) * 2,
            [VMEM] * 11, (VMEM,) * 2,
            [pltpu.VMEM((2048, 256), BF16)] * 2 + [pltpu.VMEM((512, 256), F32)],
            12, 3 << 29, 6 << 20,
            xh, xl, *blocks,
        )
        for half in range(2):
            e = TARGETS[group * 2 + half]
            sums[e] = shift("x", NX, e)(partial[half]) if e else partial[half]

    line = [own] + [shift("x", NX, r)(own) for r in range(1, NX)]
    factors = []
    for r in range(NX):
        factors += [line[r], swap()(line[r])]
    rh, rl = call(
        line_kernel, (shape(512, 1024, dtype=BF16),) * 2, [VMEM] * 8, (VMEM,) * 2, [], 8, 1 << 22, 4 << 20, *factors,
    )
    weighted, keep, send = call(
        gram_kernel, (shape(32, 64, 128), shape(4, 2, 8, 512), shape(4, 2, 8, 512)),
        [SMEM] * 2 + [VMEM] * 6, (VMEM,) * 3,
        [pltpu.VMEM((128, 512), BF16)] * 2 + [pltpu.VMEM((2, 64, 512), F32)], 8, 1 << 29, 4 << 20,
        live, weights, *[sums[e] for e in range(NX)], rh, rl,
    )
    got = permute("z", [(i, i ^ 1) for i in range(NZ)])(send)
    quads = call(
        pair_kernel, (shape(2, 8, 512),) * 4, [VMEM] * 2, (VMEM,) * 4, [], 4, 1 << 17, 1 << 19, keep, got,
    )
    quads = [quads[0]] + [shift("z", NZ, 2 * d)(quads[d]) for d in range(1, 4)]
    terms = call(
        diagonal_kernel, shape(2, 8, 512), [SMEM] + [VMEM] * 5, VMEM, [], 4, 1 << 18, 1 << 19,
        weights, *quads, diag_inverse[0],
    )
    rest = [shift("y", NY, dy)(terms) for dy in range(1, NY)]

    home = lax.all_to_all(weighted, ("y", "x", "k"), 0, 0, tiled=True)
    density_off = call(home_kernel, shape(2, 64, 512), [VMEM], VMEM, [], 8, 1 << 18, 3 << 19, home)
    density_off, *rest = lax.optimization_barrier((density_off, *rest))
    density_diag = (terms + rest[0]) + (rest[1] + rest[2])
    return density_off, density_diag


def solution(mesh):
    inner = Mesh(mesh.devices.reshape(NY, NX, NZ, NK), ("y", "x", "z", "k"))
    grid = ("x", "z", "k")
    placed = (
        P("y", None, grid, None),
        P("y", None, grid, None),
        P("y", None, grid, None),
        P("y", None),
        P(),
        P(),
    )

    return jax.shard_map(
        per_device,
        mesh=inner,
        in_specs=placed,
        out_specs=(P(None, grid, None), P(None, grid, None)),
        check_vma=False,
    )
```

```python
import functools

import jax
import jax.numpy as jnp
from jax import lax
from jax.experimental import pallas as pl
from jax.experimental.pallas import tpu as pltpu
from jax.sharding import Mesh, PartitionSpec as P


F32 = jnp.float32
BF16 = jnp.bfloat16
NX, NZ, NK, NY = 4, 8, 2, 4
OFFSETS = (0, 1, -1, 2, -2, 3, -3, 4)

TARGETS = (2, 1, 3, 0)
COLUMNS, TILES = 14 * 128, 8 * 128

SMEM = pl.BlockSpec(memory_space=pltpu.SMEM)
HBM = pl.BlockSpec(memory_space=pltpu.HBM)
VMEM = pl.BlockSpec(memory_space=pltpu.VMEM)


def shape(*dims, dtype=F32):
    return jax.ShapeDtypeStruct(dims, dtype)


def call(kernel, out_shape, in_specs, out_specs, scratch, mib, flops, nbytes, *args):
    return pl.pallas_call(
        kernel,
        out_shape=out_shape,
        in_specs=in_specs,
        out_specs=out_specs,
        scratch_shapes=scratch,
        cost_estimate=pl.CostEstimate(flops=flops, bytes_accessed=nbytes, transcendentals=0),
        compiler_params=pltpu.CompilerParams(vmem_limit_bytes=mib << 20),
    )(*args)


def split(value):
    high = value.astype(BF16)
    return high, (value - high.astype(F32)).astype(BF16)


def interleave(upper, odd, real, imag):
    same = jnp.where(upper == 0, real, imag)
    cross = pltpu.roll(jnp.where(upper == 0, imag, real), 64, 1)
    return jnp.where(upper == odd, same, cross)


def other_core(k, other):
    return k + other - 2 * k * other


def lanes_below(limit, rows=64):
    return lax.broadcasted_iota(jnp.int32, (rows, 128), 1) < limit


def one_hot(size, source):
    row = lax.broadcasted_iota(jnp.int32, (size, size), 0)
    column = lax.broadcasted_iota(jnp.int32, (size, size), 1)
    return jnp.where(row == source(column), 1.0, 0.0).astype(BF16)


def mask_kernel(
    owner_hbm, counts_hbm, factor_hbm, own, mine, theirs, live, owner, counts, factor, sems
):
    copies = [
        pltpu.make_async_copy(source, target, sems.at[i])
        for i, (source, target) in enumerate(
            ((owner_hbm, owner), (counts_hbm, counts), (factor_hbm, factor))
        )
    ]
    for copy in copies:
        copy.start()
    x, z, k = lax.axis_index("x"), lax.axis_index("z"), lax.axis_index("k")
    spots = [
        (lax.rem(x - r + NX, NX) * NZ + z) * NK + other_core(k, other) for r in range(NX) for other in range(NK)
    ]
    select = one_hot(128, lambda m: m % 64 // 8 * 16 + other_core(k, m // 64) * 8 + m % 8)
    copies[0].wait()
    copies[1].wait()

    def body(b, found):
        at, rows = owner[b], counts[b]
        return tuple(jnp.where(at == spot, rows, have) for spot, have in zip(spots, found))

    found = lax.fori_loop(0, 64, body, (jnp.int32(0),) * 8, unroll=8)
    for r in range(8):
        live[r] = found[r]
    keep = lax.broadcasted_iota(jnp.int32, (64, 512), 0) < found[0]
    copies[2].wait()
    for part in range(2):
        own[part] = jnp.where(keep, factor[part], 0.0)
    lower = lanes_below(64)
    for part in range(2):
        for q in range(2):
            turned = []
            for target in TARGETS[q * 2 : q * 2 + 2]:
                start = pl.multiple_of(lax.rem(x + target, NX) * 128, 128)
                high, low = split(own[part, :, pl.ds(start, 128)])
                turned.append(
                    jnp.dot(high, select, preferred_element_type=F32) + jnp.dot(low, select, preferred_element_type=F32)
                )
            lanes = slice(q * 128, (q + 1) * 128)
            mine[part, :, lanes] = jnp.where(lower, turned[0], pltpu.roll(turned[1], 64, 1))
            theirs[part, :, lanes] = jnp.where(lower, pltpu.roll(turned[0], 64, 1), turned[1])


def merge_kernel(first, second, out):
    out[0] = first[...]
    out[1] = second[...]


def find_blocks(owner, natural):
    def body(b, carry):
        natural[owner[b]] = b
        return carry

    lax.fori_loop(0, 64, body, 0, unroll=8)
    x, z, k = lax.axis_index("x"), lax.axis_index("z"), lax.axis_index("k")
    upper = lax.broadcasted_iota(jnp.int32, (64, 128), 1) // 64

    def tile(inverse, dx, offset, other):
        stored = lax.rem(x + dx, NX) * (NZ * NK) + lax.rem(z + offset + NZ, NZ) * NK + other_core(k, other)
        block = natural[stored]
        start = pl.multiple_of((block // 2) * 128, 128)
        return interleave(
            upper, lax.rem(block, 2), inverse[0, :, pl.ds(start, 128)], inverse[1, :, pl.ds(start, 128)]
        )

    return tile


def columns_kernel(owner_hbm, inverse_hbm, *refs):
    outs, (owner, natural, inverse, made, sems) = refs[: NX - 1], refs[NX - 1 :]
    read = pltpu.make_async_copy(owner_hbm, owner, sems.at[0])
    fill = pltpu.make_async_copy(inverse_hbm, inverse, sems.at[1])
    fill.start()
    read.start()
    read.wait()
    tile = find_blocks(owner, natural)
    fill.wait()
    writes = []
    for dx in (1, 3, 2):
        for j, offset in enumerate(OFFSETS[1:]):
            for other in range(NK):
                t = j * NK + other
                made[dx - 1, :, t * 128 : (t + 1) * 128] = tile(inverse, dx, offset, other)
        writes.append(pltpu.make_async_copy(made.at[dx - 1], outs[dx - 1], sems.at[1 + dx]))
        writes[-1].start()
    for write in writes:
        write.wait()


def own_columns_kernel(owner, inverse, out, natural):
    tile = find_blocks(owner, natural)
    lower = lanes_below(64)
    for j, offset in enumerate(OFFSETS[1:]):
        for other in range(NK):
            t = j * NK + other
            out[:, t * 128 : (t + 1) * 128] = tile(inverse, 0, offset, other)
    for r in range(NX):
        both = jnp.concatenate([tile(inverse, NX - r, 0, other) for other in range(NK)], axis=0).T
        at = COLUMNS + r * 256
        out[:, at : at + 128] = jnp.where(lower, both[:64], pltpu.roll(both[64:], 64, 1))
        out[:, at + 128 : at + 256] = jnp.where(lower, pltpu.roll(both[:64], 64, 1), both[64:])


def halve_rows(pieces, xh, xl, first):
    for i, piece in enumerate(pieces):
        rows = slice((first + i) * 64, (first + i + 1) * 64)
        for t in range(2, 16):
            at = (t if i % 2 == 0 else t + 1 - 2 * (t % 2)) - 2
            high, low = split(piece[:, at * 128 : (at + 1) * 128])
            xh[rows, t * 128 : (t + 1) * 128] = high
            xl[rows, t * 128 : (t + 1) * 128] = low


def own_rows_kernel(own, mate, xh, xl, th, tl):
    halve_rows((own, mate), xh, xl, 0)
    for block in range(8):
        rows = slice(block * 64, (block + 1) * 64)
        for t, (source, tile) in enumerate(((own, block), (mate, block + 1 - 2 * (block % 2)))):
            at = COLUMNS + tile * 128
            high, low = split(source[:, at : at + 128])
            th[rows, t * 128 : (t + 1) * 128] = high
            tl[rows, t * 128 : (t + 1) * 128] = low


def rows_kernel(own_h, own_l, tiles_h, tiles_l, *refs):
    pieces, (xh, xl) = refs[:6], refs[6:]
    for out, own, tiles in ((xh, own_h, tiles_h), (xl, own_l, tiles_l)):
        out[0:128, 256:2048] = own[:, 256:2048]
        out[:, 0:256] = tiles[...]
    halve_rows(pieces, xh, xl, 2)


def product_kernel(group, xh, xl, *refs):
    blocks, outs = refs[:9], refs[9:11]
    rh, rl, total = refs[11:]
    lanes = slice(group * 128, (group + 1) * 128)
    for t in range(16):
        rows_real, rows_imag = slice(t * 128, t * 128 + 64), slice(t * 128 + 64, t * 128 + 128)
        block = blocks[t // 2].at[t % 2] if t < 14 else blocks[t - 7].at[0]
        (real_h, real_l), (imag_h, imag_l) = split(block[0, :, lanes]), split(block[1, :, lanes])
        for out, re, im in ((rh, real_h, imag_h), (rl, real_l, imag_l)):
            out[rows_real, 0:128] = re
            out[rows_real, 128:256] = im
            out[rows_imag, 0:128] = -im
            out[rows_imag, 128:256] = re
    sums = jnp.dot(xh[...], rh[...], preferred_element_type=F32)
    sums += jnp.dot(xl[...], rh[...], preferred_element_type=F32)
    sums += jnp.dot(xh[...], rl[...], preferred_element_type=F32)
    total[...] = sums
    lower = lanes_below(64)
    for i in range(8):
        real = total[i * 64 : (i + 1) * 64, 0:128]
        imag = total[i * 64 : (i + 1) * 64, 128:256]
        for half, value in enumerate(
            (jnp.where(lower, real, pltpu.roll(imag, 64, 1)), jnp.where(lower, pltpu.roll(real, 64, 1), imag))
        ):
            e = TARGETS[group * 2 + half]
            outs[half][(e + i // 2) % NX * 2 + i % 2] = value


def line_kernel(*refs):
    factors, (rh, rl) = refs[:8], refs[8:]
    for i in range(8):
        for part in range(2):
            high, low = split(factors[i][part])
            rh[i * 64 : (i + 1) * 64, part * 512 : (part + 1) * 512] = high
            rl[i * 64 : (i + 1) * 64, part * 512 : (part + 1) * 512] = low


def gram_kernel(live, weights, p0, p1, p2, p3, rh, rl, weighted, keep, send, gh, gl, total):
    x, z, k = lax.axis_index("x"), lax.axis_index("z"), lax.axis_index("k")
    wr, wi = weights[0], weights[1]
    row = lax.broadcasted_iota(jnp.int32, (64, 128), 0)
    lower = lanes_below(64)
    for r in range(NX):
        tiles = []
        for other in range(NK):
            i = r * 2 + other
            value = jnp.where(row < live[i], -(p0[i] + p1[i] + p2[i] + p3[i]), 0.0)
            turned = pltpu.roll(value, 64, 1)
            value = wr * value + wi * jnp.where(lower, -turned, turned)
            home = lax.rem(x - r + NX, NX) * NK + other_core(k, other)
            for y in range(NY):
                weighted[y * 8 + home] = value
            tiles.append(value)
        high, low = split(jnp.concatenate(tiles, axis=0).T)
        gh[:, r * 128 : (r + 1) * 128] = high
        gl[:, r * 128 : (r + 1) * 128] = low
    halves = []
    for part in range(2):
        cols = slice(part * 512, (part + 1) * 512)
        sums = jnp.dot(gh[...], rh[:, cols], preferred_element_type=F32)
        sums += jnp.dot(gl[...], rh[:, cols], preferred_element_type=F32)
        sums += jnp.dot(gh[...], rl[:, cols], preferred_element_type=F32)
        halves.append(sums)
    total[0] = halves[0][:64] - halves[1][64:]
    total[1] = halves[1][:64] + halves[0][64:]
    odd = lax.rem(z, 2)
    for h in range(4):
        for part in range(2):
            keep[h, part] = total[part, pl.ds(pl.multiple_of(h * 16 + odd * 8, 8), 8), :]
            send[h, part] = total[part, pl.ds(pl.multiple_of(h * 16 + 8 - odd * 8, 8), 8), :]


def pair_kernel(keep, got, *outs):
    h = lax.axis_index("z") // 2
    for d in range(4):
        at = lax.rem(h + d, 4)
        outs[d][...] = keep[at] + got[at]


def diagonal_kernel(weights, s0, s1, s2, s3, diag, out):
    wr, wi = weights[0], weights[1]
    real, imag = diag[0], diag[1]
    terms = (wr * real - wi * imag, wr * imag + wi * real)
    for part in range(2):
        out[part] = terms[part] - (s0[part] + s1[part] + s2[part] + s3[part])


def home_kernel(pieces, out):
    select = one_hot(256, lambda m: m // 8 % 2 * 128 + m // 128 * 64 + m % 128 // 16 * 8 + m % 8)
    rows = []
    for x in range(NX):
        cores = []
        for k in range(NK):
            i = x * NK + k
            cores.append((pieces[i] + pieces[8 + i]) + (pieces[16 + i] + pieces[24 + i]))
        rows.append(jnp.concatenate(cores, axis=1))
    value = jnp.concatenate(rows, axis=0)
    high, rest = value.astype(BF16), None
    rest = value - high.astype(F32)
    middle, low = split(rest)
    total = jnp.dot(low, select, preferred_element_type=F32)
    total += jnp.dot(middle, select, preferred_element_type=F32)
    total += jnp.dot(high, select, preferred_element_type=F32)
    for x in range(NX):
        for part in range(2):
            out[part, :, x * 128 : (x + 1) * 128] = total[x * 64 : (x + 1) * 64, part * 128 : (part + 1) * 128]


def permute(axis, pairs):
    def go(value):
        return lax.ppermute(value, axis, pairs)

    return go


def shift(axis, size, step):
    return permute(axis, [(i, (i + step) % size) for i in range(size)])


def swap():
    return shift("k", NK, 1)


def per_device(inverse_block, factor_block, diag_inverse, residues, block_owner, row_count):
    weights = residues[0]
    own, mine, theirs, live = call(
        mask_kernel,
        (shape(2, 64, 512), shape(2, 64, 256), shape(2, 64, 256), shape(8, dtype=jnp.int32)),
        [HBM] * 3, (VMEM,) * 3 + (SMEM,),
        [pltpu.SMEM((64,), jnp.int32)] * 2 + [pltpu.VMEM((2, 64, 512), F32), pltpu.SemaphoreType.DMA((3,))],
        60, 1 << 20, 1 << 20,
        block_owner, row_count, factor_block[0],
    )
    ring = {
        0: call(merge_kernel, shape(2, 2, 64, 256), [VMEM] * 2, VMEM, [], 4, 1 << 10, 1 << 19, mine, swap()(theirs))
    }
    for step in (1, 2, 3):
        ring[step] = shift("z", NZ, -1)(ring[step - 1])
        ring[-step] = shift("z", NZ, 1)(ring[1 - step])
    last = [shift("z", NZ, -1)(ring[3][:1]), shift("z", NZ, 1)(ring[-3][1:])]
    blocks = [ring[offset] for offset in OFFSETS[:-1]] + last

    sent = call(
        columns_kernel, (shape(64, COLUMNS),) * 3, [HBM] * 2, (HBM,) * 3,
        [pltpu.SMEM((64,), jnp.int32)] * 2
        + [pltpu.VMEM((2, 64, 4096), F32), pltpu.VMEM((3, 64, COLUMNS), F32), pltpu.SemaphoreType.DMA((5,))],
        60, 1 << 20, 4 << 20,
        block_owner, inverse_block[0],
    )
    pieces = [
        call(
            own_columns_kernel, shape(64, COLUMNS + TILES), [SMEM, VMEM], VMEM,
            [pltpu.SMEM((64,), jnp.int32)], 6, 1 << 20, 3 << 20,
            block_owner, inverse_block[0],
        ),
        *sent,
    ]
    rows = {0: pieces[0]}
    for dx in (1, 3, 2):
        rows[dx] = shift("x", NX, dx)(pieces[dx])
    both = []
    for dx in range(NX):
        both += [rows[dx], swap()(rows[dx])]
    halves = call(
        own_rows_kernel, (shape(128, 2048, dtype=BF16),) * 2 + (shape(512, 256, dtype=BF16),) * 2,
        [VMEM] * 2, (VMEM,) * 4, [], 4, 1 << 20, 3 << 20, *both[:2],
    )
    xh, xl = call(
        rows_kernel, (shape(512, 2048, dtype=BF16),) * 2, [VMEM] * 10, (VMEM,) * 2, [], 16, 1 << 22, 8 << 20,
        *halves, *both[2:],
    )
    sums = {}
    for group in range(2):
        partial = call(
            functools.partial(product_kernel, group), (shape(8, 64, 128),) * 2,
            [VMEM] * 11, (VMEM,) * 2,
            [pltpu.VMEM((2048, 256), BF16)] * 2 + [pltpu.VMEM((512, 256), F32)],
            12, 3 << 29, 6 << 20,
            xh, xl, *blocks,
        )
        for half in range(2):
            e = TARGETS[group * 2 + half]
            sums[e] = shift("x", NX, e)(partial[half]) if e else partial[half]

    line = [own] + [shift("x", NX, r)(own) for r in range(1, NX)]
    factors = []
    for r in range(NX):
        factors += [line[r], swap()(line[r])]
    rh, rl = call(
        line_kernel, (shape(512, 1024, dtype=BF16),) * 2, [VMEM] * 8, (VMEM,) * 2, [], 8, 1 << 22, 4 << 20, *factors,
    )
    weighted, keep, send = call(
        gram_kernel, (shape(32, 64, 128), shape(4, 2, 8, 512), shape(4, 2, 8, 512)),
        [SMEM] * 2 + [VMEM] * 6, (VMEM,) * 3,
        [pltpu.VMEM((128, 512), BF16)] * 2 + [pltpu.VMEM((2, 64, 512), F32)], 8, 1 << 29, 4 << 20,
        live, weights, *[sums[e] for e in range(NX)], rh, rl,
    )
    got = permute("z", [(i, i ^ 1) for i in range(NZ)])(send)
    quads = call(
        pair_kernel, (shape(2, 8, 512),) * 4, [VMEM] * 2, (VMEM,) * 4, [], 4, 1 << 17, 1 << 19, keep, got,
    )
    quads = [quads[0]] + [shift("z", NZ, 2 * d)(quads[d]) for d in range(1, 4)]
    terms = call(
        diagonal_kernel, shape(2, 8, 512), [SMEM] + [VMEM] * 5, VMEM, [], 4, 1 << 18, 1 << 19,
        weights, *quads, diag_inverse[0],
    )
    rest = [shift("y", NY, dy)(terms) for dy in range(1, NY)]

    home = lax.all_to_all(weighted, ("y", "x", "k"), 0, 0, tiled=True)
    density_off = call(home_kernel, shape(2, 64, 512), [VMEM], VMEM, [], 8, 1 << 18, 3 << 19, home)
    density_off, *rest = lax.optimization_barrier((density_off, *rest))
    density_diag = (terms + rest[0]) + (rest[1] + rest[2])
    return density_off, density_diag


def solution(mesh):
    inner = Mesh(mesh.devices.reshape(NY, NX, NZ, NK), ("y", "x", "z", "k"))
    grid = ("x", "z", "k")
    placed = (
        P("y", None, grid, None),
        P("y", None, grid, None),
        P("y", None, grid, None),
        P("y", None),
        P(),
        P(),
    )

    return jax.shard_map(
        per_device,
        mesh=inner,
        in_specs=placed,
        out_specs=(P(None, grid, None), P(None, grid, None)),
        check_vma=False,
    )
```

```python
import functools

import jax
import jax.numpy as jnp
from jax import lax
from jax.experimental import pallas as pl
from jax.experimental.pallas import tpu as pltpu
from jax.sharding import Mesh, PartitionSpec as P


F32 = jnp.float32
BF16 = jnp.bfloat16
NX, NZ, NK, NY = 4, 8, 2, 4
OFFSETS = (0, 1, -1, 2, -2, 3, -3, 4)

TARGETS = (2, 1, 3, 0)
COLUMNS, TILES = 14 * 128, 8 * 128

SMEM = pl.BlockSpec(memory_space=pltpu.SMEM)
HBM = pl.BlockSpec(memory_space=pltpu.HBM)
VMEM = pl.BlockSpec(memory_space=pltpu.VMEM)


def shape(*dims, dtype=F32):
    return jax.ShapeDtypeStruct(dims, dtype)


def call(kernel, out_shape, in_specs, out_specs, scratch, mib, flops, nbytes, *args):
    return pl.pallas_call(
        kernel,
        out_shape=out_shape,
        in_specs=in_specs,
        out_specs=out_specs,
        scratch_shapes=scratch,
        cost_estimate=pl.CostEstimate(flops=flops, bytes_accessed=nbytes, transcendentals=0),
        compiler_params=pltpu.CompilerParams(vmem_limit_bytes=mib << 20),
    )(*args)


def split(value):
    high = value.astype(BF16)
    return high, (value - high.astype(F32)).astype(BF16)


def interleave(upper, odd, real, imag):
    same = jnp.where(upper == 0, real, imag)
    cross = pltpu.roll(jnp.where(upper == 0, imag, real), 64, 1)
    return jnp.where(upper == odd, same, cross)


def other_core(k, other):
    return k + other - 2 * k * other


def lanes_below(limit, rows=64):
    return lax.broadcasted_iota(jnp.int32, (rows, 128), 1) < limit


def one_hot(size, source):
    row = lax.broadcasted_iota(jnp.int32, (size, size), 0)
    column = lax.broadcasted_iota(jnp.int32, (size, size), 1)
    return jnp.where(row == source(column), 1.0, 0.0).astype(BF16)


def mask_kernel(
    owner_hbm, counts_hbm, factor_hbm, own, mine, theirs, live, owner, counts, factor, sems
):
    copies = [
        pltpu.make_async_copy(source, target, sems.at[i])
        for i, (source, target) in enumerate(
            ((owner_hbm, owner), (counts_hbm, counts), (factor_hbm, factor))
        )
    ]
    for copy in copies:
        copy.start()
    x, z, k = lax.axis_index("x"), lax.axis_index("z"), lax.axis_index("k")
    spots = [
        (lax.rem(x - r + NX, NX) * NZ + z) * NK + other_core(k, other) for r in range(NX) for other in range(NK)
    ]
    select = one_hot(128, lambda m: m % 64 // 8 * 16 + other_core(k, m // 64) * 8 + m % 8)
    copies[0].wait()
    copies[1].wait()

    def body(b, found):
        at, rows = owner[b], counts[b]
        return tuple(jnp.where(at == spot, rows, have) for spot, have in zip(spots, found))

    found = lax.fori_loop(0, 64, body, (jnp.int32(0),) * 8, unroll=8)
    for r in range(8):
        live[r] = found[r]
    keep = lax.broadcasted_iota(jnp.int32, (64, 512), 0) < found[0]
    copies[2].wait()
    for part in range(2):
        own[part] = jnp.where(keep, factor[part], 0.0)
    lower = lanes_below(64)
    for part in range(2):
        for q in range(2):
            turned = []
            for target in TARGETS[q * 2 : q * 2 + 2]:
                start = pl.multiple_of(lax.rem(x + target, NX) * 128, 128)
                high, low = split(own[part, :, pl.ds(start, 128)])
                turned.append(
                    jnp.dot(high, select, preferred_element_type=F32) + jnp.dot(low, select, preferred_element_type=F32)
                )
            lanes = slice(q * 128, (q + 1) * 128)
            mine[part, :, lanes] = jnp.where(lower, turned[0], pltpu.roll(turned[1], 64, 1))
            theirs[part, :, lanes] = jnp.where(lower, pltpu.roll(turned[0], 64, 1), turned[1])


def merge_kernel(first, second, out):
    out[0] = first[...]
    out[1] = second[...]


def find_blocks(owner, natural):
    def body(b, carry):
        natural[owner[b]] = b
        return carry

    lax.fori_loop(0, 64, body, 0, unroll=8)
    x, z, k = lax.axis_index("x"), lax.axis_index("z"), lax.axis_index("k")
    upper = lax.broadcasted_iota(jnp.int32, (64, 128), 1) // 64

    def tile(inverse, dx, offset, other):
        stored = lax.rem(x + dx, NX) * (NZ * NK) + lax.rem(z + offset + NZ, NZ) * NK + other_core(k, other)
        block = natural[stored]
        start = pl.multiple_of((block // 2) * 128, 128)
        return interleave(
            upper, lax.rem(block, 2), inverse[0, :, pl.ds(start, 128)], inverse[1, :, pl.ds(start, 128)]
        )

    return tile


def columns_kernel(owner_hbm, inverse_hbm, *refs):
    outs, (owner, natural, inverse, made, sems) = refs[: NX - 1], refs[NX - 1 :]
    read = pltpu.make_async_copy(owner_hbm, owner, sems.at[0])
    fill = pltpu.make_async_copy(inverse_hbm, inverse, sems.at[1])
    fill.start()
    read.start()
    read.wait()
    tile = find_blocks(owner, natural)
    fill.wait()
    writes = []
    for dx in (1, 3, 2):
        for j, offset in enumerate(OFFSETS[1:]):
            for other in range(NK):
                t = j * NK + other
                made[dx - 1, :, t * 128 : (t + 1) * 128] = tile(inverse, dx, offset, other)
        writes.append(pltpu.make_async_copy(made.at[dx - 1], outs[dx - 1], sems.at[1 + dx]))
        writes[-1].start()
    for write in writes:
        write.wait()


def own_columns_kernel(owner, inverse, out, natural):
    tile = find_blocks(owner, natural)
    lower = lanes_below(64)
    for j, offset in enumerate(OFFSETS[1:]):
        for other in range(NK):
            t = j * NK + other
            out[:, t * 128 : (t + 1) * 128] = tile(inverse, 0, offset, other)
    for r in range(NX):
        both = jnp.concatenate([tile(inverse, NX - r, 0, other) for other in range(NK)], axis=0).T
        at = COLUMNS + r * 256
        out[:, at : at + 128] = jnp.where(lower, both[:64], pltpu.roll(both[64:], 64, 1))
        out[:, at + 128 : at + 256] = jnp.where(lower, pltpu.roll(both[:64], 64, 1), both[64:])


def halve_rows(pieces, xh, xl, first):
    for i, piece in enumerate(pieces):
        rows = slice((first + i) * 64, (first + i + 1) * 64)
        for t in range(2, 16):
            at = (t if i % 2 == 0 else t + 1 - 2 * (t % 2)) - 2
            high, low = split(piece[:, at * 128 : (at + 1) * 128])
            xh[rows, t * 128 : (t + 1) * 128] = high
            xl[rows, t * 128 : (t + 1) * 128] = low


def own_rows_kernel(own, mate, xh, xl, th, tl):
    halve_rows((own, mate), xh, xl, 0)
    for block in range(8):
        rows = slice(block * 64, (block + 1) * 64)
        for t, (source, tile) in enumerate(((own, block), (mate, block + 1 - 2 * (block % 2)))):
            at = COLUMNS + tile * 128
            high, low = split(source[:, at : at + 128])
            th[rows, t * 128 : (t + 1) * 128] = high
            tl[rows, t * 128 : (t + 1) * 128] = low


def rows_kernel(own_h, own_l, tiles_h, tiles_l, *refs):
    pieces, (xh, xl) = refs[:6], refs[6:]
    for out, own, tiles in ((xh, own_h, tiles_h), (xl, own_l, tiles_l)):
        out[0:128, 256:2048] = own[:, 256:2048]
        out[:, 0:256] = tiles[...]
    halve_rows(pieces, xh, xl, 2)


def product_kernel(group, xh, xl, *refs):
    blocks, outs = refs[:9], refs[9:11]
    rh, rl, total = refs[11:]
    lanes = slice(group * 128, (group + 1) * 128)
    for t in range(16):
        rows_real, rows_imag = slice(t * 128, t * 128 + 64), slice(t * 128 + 64, t * 128 + 128)
        block = blocks[t // 2].at[t % 2] if t < 14 else blocks[t - 7].at[0]
        (real_h, real_l), (imag_h, imag_l) = split(block[0, :, lanes]), split(block[1, :, lanes])
        for out, re, im in ((rh, real_h, imag_h), (rl, real_l, imag_l)):
            out[rows_real, 0:128] = re
            out[rows_real, 128:256] = im
            out[rows_imag, 0:128] = -im
            out[rows_imag, 128:256] = re
    sums = jnp.dot(xh[...], rh[...], preferred_element_type=F32)
    sums += jnp.dot(xl[...], rh[...], preferred_element_type=F32)
    sums += jnp.dot(xh[...], rl[...], preferred_element_type=F32)
    total[...] = sums
    lower = lanes_below(64)
    for i in range(8):
        real = total[i * 64 : (i + 1) * 64, 0:128]
        imag = total[i * 64 : (i + 1) * 64, 128:256]
        for half, value in enumerate(
            (jnp.where(lower, real, pltpu.roll(imag, 64, 1)), jnp.where(lower, pltpu.roll(real, 64, 1), imag))
        ):
            e = TARGETS[group * 2 + half]
            outs[half][(e + i // 2) % NX * 2 + i % 2] = value


def line_kernel(*refs):
    factors, (rh, rl) = refs[:8], refs[8:]
    for i in range(8):
        for part in range(2):
            high, low = split(factors[i][part])
            rh[i * 64 : (i + 1) * 64, part * 512 : (part + 1) * 512] = high
            rl[i * 64 : (i + 1) * 64, part * 512 : (part + 1) * 512] = low


def gram_kernel(live, weights, p0, p1, p2, p3, rh, rl, weighted, keep, send, gh, gl, total):
    x, z, k = lax.axis_index("x"), lax.axis_index("z"), lax.axis_index("k")
    wr, wi = weights[0], weights[1]
    row = lax.broadcasted_iota(jnp.int32, (64, 128), 0)
    lower = lanes_below(64)
    for r in range(NX):
        tiles = []
        for other in range(NK):
            i = r * 2 + other
            value = jnp.where(row < live[i], -(p0[i] + p1[i] + p2[i] + p3[i]), 0.0)
            turned = pltpu.roll(value, 64, 1)
            value = wr * value + wi * jnp.where(lower, -turned, turned)
            for y in range(NY):
                weighted[y * 4 + lax.rem(x - r + NX, NX), other_core(k, other)] = value
            tiles.append(value)
        high, low = split(jnp.concatenate(tiles, axis=0).T)
        gh[:, r * 128 : (r + 1) * 128] = high
        gl[:, r * 128 : (r + 1) * 128] = low
    halves = []
    for part in range(2):
        cols = slice(part * 512, (part + 1) * 512)
        sums = jnp.dot(gh[...], rh[:, cols], preferred_element_type=F32)
        sums += jnp.dot(gl[...], rh[:, cols], preferred_element_type=F32)
        sums += jnp.dot(gh[...], rl[:, cols], preferred_element_type=F32)
        halves.append(sums)
    total[0] = halves[0][:64] - halves[1][64:]
    total[1] = halves[1][:64] + halves[0][64:]
    odd = lax.rem(z, 2)
    for h in range(4):
        for part in range(2):
            keep[h, part] = total[part, pl.ds(pl.multiple_of(h * 16 + odd * 8, 8), 8), :]
            send[h, part] = total[part, pl.ds(pl.multiple_of(h * 16 + 8 - odd * 8, 8), 8), :]


def pair_kernel(keep, got, *outs):
    h = lax.axis_index("z") // 2
    for d in range(4):
        at = lax.rem(h + d, 4)
        outs[d][...] = keep[at] + got[at]


def diagonal_kernel(weights, s0, s1, s2, s3, diag, out):
    wr, wi = weights[0], weights[1]
    real, imag = diag[0], diag[1]
    terms = (wr * real - wi * imag, wr * imag + wi * real)
    for part in range(2):
        out[part] = terms[part] - (s0[part] + s1[part] + s2[part] + s3[part])


def gather_kernel(pieces, keep, send):
    k = lax.axis_index("k")
    for x in range(NX):
        for out, core in ((keep, k), (send, 1 - k)):
            out[x] = (pieces[x, core] + pieces[4 + x, core]) + (pieces[8 + x, core] + pieces[12 + x, core])


def home_kernel(keep, got, out):
    first = lax.axis_index("k") == 0
    select = one_hot(256, lambda m: m // 8 % 2 * 128 + m // 128 * 64 + m % 128 // 16 * 8 + m % 8)
    rows = []
    for x in range(NX):
        cores = [jnp.where(first, keep[x], got[x]), jnp.where(first, got[x], keep[x])]
        rows.append(jnp.concatenate(cores, axis=1))
    value = jnp.concatenate(rows, axis=0)
    high = value.astype(BF16)
    middle, low = split(value - high.astype(F32))
    total = jnp.dot(low, select, preferred_element_type=F32)
    total += jnp.dot(middle, select, preferred_element_type=F32)
    total += jnp.dot(high, select, preferred_element_type=F32)
    for x in range(NX):
        for part in range(2):
            out[part, :, x * 128 : (x + 1) * 128] = total[x * 64 : (x + 1) * 64, part * 128 : (part + 1) * 128]


def permute(axis, pairs):
    def go(value):
        return lax.ppermute(value, axis, pairs)

    return go


def shift(axis, size, step):
    return permute(axis, [(i, (i + step) % size) for i in range(size)])


def swap():
    return shift("k", NK, 1)


def per_device(inverse_block, factor_block, diag_inverse, residues, block_owner, row_count):
    weights = residues[0]
    own, mine, theirs, live = call(
        mask_kernel,
        (shape(2, 64, 512), shape(2, 64, 256), shape(2, 64, 256), shape(8, dtype=jnp.int32)),
        [HBM] * 3, (VMEM,) * 3 + (SMEM,),
        [pltpu.SMEM((64,), jnp.int32)] * 2 + [pltpu.VMEM((2, 64, 512), F32), pltpu.SemaphoreType.DMA((3,))],
        60, 1 << 20, 1 << 20,
        block_owner, row_count, factor_block[0],
    )
    ring = {
        0: call(merge_kernel, shape(2, 2, 64, 256), [VMEM] * 2, VMEM, [], 4, 1 << 10, 1 << 19, mine, swap()(theirs))
    }
    for step in (1, 2, 3):
        ring[step] = shift("z", NZ, -1)(ring[step - 1])
        ring[-step] = shift("z", NZ, 1)(ring[1 - step])
    last = [shift("z", NZ, -1)(ring[3][:1]), shift("z", NZ, 1)(ring[-3][1:])]
    blocks = [ring[offset] for offset in OFFSETS[:-1]] + last

    sent = call(
        columns_kernel, (shape(64, COLUMNS),) * 3, [HBM] * 2, (HBM,) * 3,
        [pltpu.SMEM((64,), jnp.int32)] * 2
        + [pltpu.VMEM((2, 64, 4096), F32), pltpu.VMEM((3, 64, COLUMNS), F32), pltpu.SemaphoreType.DMA((5,))],
        60, 1 << 20, 4 << 20,
        block_owner, inverse_block[0],
    )
    pieces = [
        call(
            own_columns_kernel, shape(64, COLUMNS + TILES), [SMEM, VMEM], VMEM,
            [pltpu.SMEM((64,), jnp.int32)], 6, 1 << 20, 3 << 20,
            block_owner, inverse_block[0],
        ),
        *sent,
    ]
    rows = {0: pieces[0]}
    for dx in (1, 3, 2):
        rows[dx] = shift("x", NX, dx)(pieces[dx])
    both = []
    for dx in range(NX):
        both += [rows[dx], swap()(rows[dx])]
    halves = call(
        own_rows_kernel, (shape(128, 2048, dtype=BF16),) * 2 + (shape(512, 256, dtype=BF16),) * 2,
        [VMEM] * 2, (VMEM,) * 4, [], 4, 1 << 20, 3 << 20, *both[:2],
    )
    xh, xl = call(
        rows_kernel, (shape(512, 2048, dtype=BF16),) * 2, [VMEM] * 10, (VMEM,) * 2, [], 16, 1 << 22, 8 << 20,
        *halves, *both[2:],
    )
    sums = {}
    for group in range(2):
        partial = call(
            functools.partial(product_kernel, group), (shape(8, 64, 128),) * 2,
            [VMEM] * 11, (VMEM,) * 2,
            [pltpu.VMEM((2048, 256), BF16)] * 2 + [pltpu.VMEM((512, 256), F32)],
            12, 3 << 29, 6 << 20,
            xh, xl, *blocks,
        )
        for half in range(2):
            e = TARGETS[group * 2 + half]
            sums[e] = shift("x", NX, e)(partial[half]) if e else partial[half]

    line = [own] + [shift("x", NX, r)(own) for r in range(1, NX)]
    factors = []
    for r in range(NX):
        factors += [line[r], swap()(line[r])]
    rh, rl = call(
        line_kernel, (shape(512, 1024, dtype=BF16),) * 2, [VMEM] * 8, (VMEM,) * 2, [], 8, 1 << 22, 4 << 20, *factors,
    )
    weighted, keep, send = call(
        gram_kernel, (shape(16, 2, 64, 128), shape(4, 2, 8, 512), shape(4, 2, 8, 512)),
        [SMEM] * 2 + [VMEM] * 6, (VMEM,) * 3,
        [pltpu.VMEM((128, 512), BF16)] * 2 + [pltpu.VMEM((2, 64, 512), F32)], 8, 1 << 29, 4 << 20,
        live, weights, *[sums[e] for e in range(NX)], rh, rl,
    )
    got = permute("z", [(i, i ^ 1) for i in range(NZ)])(send)
    quads = call(
        pair_kernel, (shape(2, 8, 512),) * 4, [VMEM] * 2, (VMEM,) * 4, [], 4, 1 << 17, 1 << 19, keep, got,
    )
    quads = [quads[0]] + [shift("z", NZ, 2 * d)(quads[d]) for d in range(1, 4)]
    terms = call(
        diagonal_kernel, shape(2, 8, 512), [SMEM] + [VMEM] * 5, VMEM, [], 4, 1 << 18, 1 << 19,
        weights, *quads, diag_inverse[0],
    )
    rest = [shift("y", NY, dy)(terms) for dy in range(1, NY)]

    home = lax.all_to_all(weighted, ("y", "x"), 0, 0, tiled=True)
    kept, given = call(
        gather_kernel, (shape(NX, 64, 128),) * 2, [VMEM], (VMEM,) * 2, [], 8, 1 << 18, 3 << 19, home,
    )
    density_off = call(home_kernel, shape(2, 64, 512), [VMEM] * 2, VMEM, [], 8, 1 << 18, 1 << 19, kept, swap()(given))
    density_off, *rest = lax.optimization_barrier((density_off, *rest))
    density_diag = (terms + rest[0]) + (rest[1] + rest[2])
    return density_off, density_diag


def solution(mesh):
    inner = Mesh(mesh.devices.reshape(NY, NX, NZ, NK), ("y", "x", "z", "k"))
    grid = ("x", "z", "k")
    placed = (
        P("y", None, grid, None),
        P("y", None, grid, None),
        P("y", None, grid, None),
        P("y", None),
        P(),
        P(),
    )

    return jax.shard_map(
        per_device,
        mesh=inner,
        in_specs=placed,
        out_specs=(P(None, grid, None), P(None, grid, None)),
        check_vma=False,
    )
```
